256 devices in a mesh: dp: 64 (over x, z, core), dim: 4 (over y).
Axes of the slice: x: 4, y: 4, z: 8, core: 2. Of those that a mesh axis runs over, the one named last changes fastest.
Arguments:
- vectors: bfloat16 [768, 65536], P('dim', 'dp'), may hold values from -30 to 30
- codes: int32 [64, 65536], P('dim', 'dp'), may hold values from 0 to 255, as said below
- codebook: bfloat16 [256, 768], P(None, 'dim'), may hold values from -4 to 4
Outputs:
- rotation: float32 [768, 768], P('dim')
- new_codebook: float32 [256, 768], P('dp', 'dim')
The draws below stay inside these ranges and needn't reach their ends.
Inputs may be any that keep to these rules, and one draw needn't show every extreme that they name: `codes`: each entry names a centroid of its subspace; in each subspace at least one centroid, which one is drawn from the seed, is named by no vector.
All inputs are finite; a program needn't handle non-finite values.
Results may differ from the reference program's by a relative error of at most 0.003.
Values may be sent and summed in bfloat16 or wider, within the bound.
A program may use at most 64 MiB of HBM per device.

```python
import math
import jax
import jax.numpy as jnp
from jax import lax

D = 768
M = 64
K = 256
NS_STEPS = 4
ROWS = 65536


def code_table(key):
    base = jax.random.fold_in(key, 701)
    unused = jax.random.randint(jax.random.fold_in(base, 1), (M, 1), 0, K)
    offsets = jax.random.randint(jax.random.fold_in(base, 2), (M, ROWS), 0, K - 1)
    return ((unused + 1 + offsets) % K).astype(jnp.int32)


def book_table(key):
    base = jax.random.fold_in(key, 702)
    values = jnp.clip(jax.random.normal(jax.random.fold_in(base, 3), (K, D), jnp.float32), -4.0, 4.0)
    return values.astype(jnp.bfloat16).astype(jnp.float32)


def draw_codes(key, part):
    return code_table(key)


def draw_codebook(key, part):
    return book_table(key).astype(jnp.bfloat16)


def draw_vectors(key, part):
    code_rows = code_table(key)
    book = book_table(key)
    index_rows = jnp.repeat(code_rows, D // M, axis=0)
    decoded = jnp.take_along_axis(book.T, index_rows, axis=1)
    scale_key = jax.random.fold_in(key, 703)
    noise_key = jax.random.fold_in(key, 704)
    feature_scale = jnp.exp(jax.random.uniform(scale_key, (D, 1), jnp.float32, math.log(0.2), math.log(5.0)))
    noise = jnp.clip(jax.random.normal(noise_key, (D, ROWS), jnp.float32), -4.0, 4.0)
    return (feature_scale * (0.5 * decoded + noise)).astype(jnp.bfloat16)


def setup_inputs(seed: int = 0) -> dict:
    splits = jax.random.split(jax.random.key(seed), 4)
    return {
        "vectors": draw_vectors(jax.random.fold_in(splits[3], 71), 0),
        "codes": draw_codes(jax.random.fold_in(splits[3], 71), 0),
        "codebook": draw_codebook(jax.random.fold_in(splits[3], 71), 0),
    }


def reference(vectors, codes, codebook):
    sub_width = D // M
    book_cube = codebook.reshape(K, M, sub_width)
    selected = book_cube[codes.T, jnp.arange(M, dtype=jnp.int32)[None, :]]
    decoded = selected.reshape(ROWS, D)
    cross = jnp.dot(vectors, decoded, preferred_element_type=jnp.float32)
    magnitude = jnp.sqrt(jnp.sum(cross * cross))
    current = cross.T / magnitude
    for iteration in range(NS_STEPS):
        gram_full = jnp.dot(current, current.T, precision=lax.Precision.HIGHEST)
        current = 1.5 * current - 0.5 * jnp.dot(gram_full, current, precision=lax.Precision.HIGHEST)
    rotation = current
    rotation_low = rotation.astype(jnp.bfloat16)
    rotated = jnp.dot(vectors.T, rotation_low.T, preferred_element_type=jnp.float32).astype(jnp.bfloat16)
    slabs = jnp.transpose(rotated.reshape(ROWS, M, sub_width), (1, 0, 2))

    def refit(operands):
        slab_rows, code_row = operands
        totals = jax.ops.segment_sum(slab_rows.astype(jnp.float32), code_row, num_segments=K)
        tallies = jax.ops.segment_sum(jnp.ones((ROWS,), jnp.float32), code_row, num_segments=K)
        return (totals, tallies)
    centroid_sums, counts = lax.map(refit, (slabs, codes))
    centroid_sums = jnp.transpose(centroid_sums, (1, 0, 2)).reshape(K, D)
    counts = jnp.repeat(counts.T, sub_width, axis=1)
    new_codebook = centroid_sums / jnp.maximum(counts, 1.0)
    return (rotation, new_codebook)
```

```python
import jax
import jax.numpy as jnp
from jax import lax
from jax.experimental import pallas as pl
from jax.experimental.pallas import tpu as pltpu
from jax.sharding import PartitionSpec as P

NX, NZ, NC, NY = 4, 8, 2, 4
D, M, K = 768, 64, 256
SUB = D // M
OWN = D // NY
OWN_M = M // NY
TILES = 18
PADDED = 24
PER_Z = PADDED // NZ
HALF = TILES // 2
MESH = pl.DeviceIdType.MESH
F32, BF16 = jnp.float32, jnp.bfloat16


def position():
    dp = lax.axis_index("dp")
    y = lax.axis_index("dim")
    core = lax.rem(dp, NC)
    z = lax.rem(dp // NC, NZ)
    x = dp // (NC * NZ)
    return x, z, core, y


def device(x, z, core, y):
    return ((x * NZ + z) * NC + core, y)


def greet(peers):
    barrier = pltpu.get_barrier_semaphore()
    for peer in peers:
        pl.semaphore_signal(barrier, inc=1, device_id=peer, device_id_type=MESH)
    pl.semaphore_wait(barrier, len(peers))


def remote(src, dst, send_sem, recv_sem, k, peer):
    return pltpu.make_async_remote_copy(
        src_ref=src,
        dst_ref=dst,
        send_sem=send_sem.at[k],
        recv_sem=recv_sem.at[k],
        device_id=peer,
        device_id_type=MESH,
    )


def gather_kernel(codes_ref, book_ref, codes_all, book_all, send_sem, recv_sem):
    x, z, core, y = position()
    peers = [device(x, z, core, lax.rem(y + off, NY)) for off in range(1, NY)]
    greet(peers)
    copies = []
    for i, peer in enumerate(peers):
        copies.append(remote(book_ref, book_all.at[y], send_sem, recv_sem, 2 * i, peer))
        copies[-1].start()
        copies.append(
            remote(codes_ref, codes_all.at[y], send_sem, recv_sem, 2 * i + 1, peer)
        )
        copies[-1].start()
    codes_all[y] = codes_ref[...]
    book_all[y] = book_ref[...]
    for copy in copies:
        copy.wait()


def gather_codes(codes, book):
    vmem = pl.BlockSpec(memory_space=pltpu.VMEM)
    return pl.pallas_call(
        gather_kernel,
        out_shape=(
            jax.ShapeDtypeStruct((NY,) + codes.shape, codes.dtype),
            jax.ShapeDtypeStruct((NY,) + book.shape, book.dtype),
        ),
        in_specs=[vmem, vmem],
        out_specs=(vmem, vmem),
        scratch_shapes=[pltpu.SemaphoreType.DMA((6,)), pltpu.SemaphoreType.DMA((6,))],
        compiler_params=pltpu.CompilerParams(collective_id=0, has_side_effects=True),
        name="gather_codes",
    )(codes, book)


def cross_kernel(codes_ref, book_ref, vectors_ref, part_ref, codes_int, decoded):
    rows = vectors_ref.shape[1]
    codes_int[...] = codes_ref[...].astype(jnp.int32)
    group = 8
    height = group * SUB
    which = lax.broadcasted_iota(jnp.int32, (height, 128), 0) // SUB

    @pl.loop(0, M // group)
    def _(g):
        base = pl.multiple_of(g * height, 16)
        book = book_ref[pl.ds(base, height), :].astype(F32)
        low, high = book[:, :128], book[:, 128:]
        for block in range(rows // 128):
            cols = pl.ds(block * 128, 128)
            lines = codes_int[pl.ds(pl.multiple_of(g * group, group), group), cols]
            index = jnp.broadcast_to(lines[0:1], (height, 128))
            for s in range(1, group):
                line = jnp.broadcast_to(lines[s : s + 1], (height, 128))
                index = jnp.where(which == s, line, index)
            lane = index & 127
            picked = jnp.where(
                index >= 128,
                jnp.take_along_axis(high, lane, axis=1),
                jnp.take_along_axis(low, lane, axis=1),
            )
            decoded[pl.ds(base, height), cols] = picked.astype(BF16)

    for pair in range(NX * NC):
        strip = lax.dot_general(
            vectors_ref[pair * 24 : pair * 24 + 24, :],
            decoded[...],
            (((1,), (1,)), ((), ())),
            preferred_element_type=F32,
        )
        for t in range(TILES):
            i, j = t // 6, t % 6
            part_ref[pair, t] = strip[i * 8 : i * 8 + 8, j * 128 : j * 128 + 128]
        for t in range(TILES, PADDED):
            part_ref[pair, t] = jnp.zeros((8, 128), F32)


def cross_part(codes_all, book_all, vectors):
    rows = vectors.shape[1]
    vmem = pl.BlockSpec(memory_space=pltpu.VMEM)
    return pl.pallas_call(
        cross_kernel,
        out_shape=jax.ShapeDtypeStruct((NX * NC, PADDED, 8, 128), F32),
        in_specs=[vmem] * 3,
        out_specs=vmem,
        scratch_shapes=[pltpu.VMEM((M, rows), jnp.int32), pltpu.VMEM((D, rows), BF16)],
        compiler_params=pltpu.CompilerParams(vmem_limit_bytes=40 * 2**20),
        name="cross_part",
    )(codes_all, book_all, vectors)


def sum_kernel(
    part_ref, vectors_ref, full, vectors_all,
    box_core, sum_core, box_x, sum_x, box_z, send_sem, recv_sem, send_vec, recv_vec,
):
    x, z, core, y = position()
    sibling = device(x, z, 1 - core, y)
    across_x = [device(lax.rem(x + off, NX), z, core, y) for off in range(1, NX)]
    across_z = [device(x, lax.rem(z + off, NZ), core, y) for off in range(1, NZ)]
    across_y = [device(x, z, core, lax.rem(y + off, NY)) for off in range(1, NY)]
    greet([sibling] + across_x + across_z + across_y)
    sent = []

    def send(src, dst, k, peer):
        copy = remote(src, dst, send_sem, recv_sem, k, peer)
        copy.start()
        sent.append(copy)
        return copy

    first = send(part_ref.at[:, 1 - core], box_core, 0, sibling)
    for i, peer in enumerate(across_y):
        copy = remote(vectors_ref, vectors_all.at[y], send_vec, recv_vec, i, peer)
        copy.start()
    vectors_all[y] = vectors_ref[...]
    first.wait_recv()
    sum_core[...] = part_ref[:, core] + box_core[...]
    stage = [
        send(sum_core.at[lax.rem(x + i + 1, NX)], box_x.at[i], 1 + i, peer)
        for i, peer in enumerate(across_x)
    ]
    for copy in stage:
        copy.wait_recv()
    sum_x[...] = (sum_core[x] + box_x[0]) + (box_x[1] + box_x[2])
    stage = [
        send(
            sum_x.at[pl.ds(lax.rem(z + i + 1, NZ) * PER_Z, PER_Z)],
            box_z.at[i], 4 + i, peer,
        )
        for i, peer in enumerate(across_z)
    ]
    for copy in stage:
        copy.wait_recv()
    mine = pl.ds(z * PER_Z, PER_Z)
    total = sum_x[mine]
    for i in range(NZ - 1):
        total = total + box_z[i]
    full[y, x, core, mine] = total

    own = full.at[y, x, core, mine]
    stage = [send(own, own, 11 + i, peer) for i, peer in enumerate(across_z)]
    for copy in stage:
        copy.wait_recv()
    one, two = pl.ds(0, HALF), pl.ds(HALF, HALF)
    stage = []
    half = full.at[y, x, core, one]
    for i, peer in enumerate(across_x):
        stage.append(send(half, half, 18 + i, peer))
    half = full.at[y, x, core, two]
    for i, peer in enumerate(across_y):
        stage.append(send(half, half, 21 + i, peer))
    for copy in stage:
        copy.wait_recv()
    line_one = full.at[y, :, core, one]
    line_two = full.at[:, x, core, two]
    last_one = [send(line_one, line_one, 24 + i, p) for i, p in enumerate(across_y)]
    last_two = [send(line_two, line_two, 27 + i, p) for i, p in enumerate(across_x)]
    final = [
        send(line_one, line_one, 30, sibling),
        send(line_two, line_two, 31, sibling),
    ]
    for i in range(NX - 1):
        last_one[i].wait_recv()
        line = full.at[lax.rem(y + NY - i - 1, NY), :, core, one]
        final.append(send(line, line, 32 + i, sibling))
        last_two[i].wait_recv()
        line = full.at[:, lax.rem(x + NX - i - 1, NX), core, two]
        final.append(send(line, line, 35 + i, sibling))
    for copy in final:
        copy.wait_recv()
    for copy in sent:
        copy.wait_send()
    for i, peer in enumerate(across_y):
        remote(vectors_ref, vectors_all.at[y], send_vec, recv_vec, i, peer).wait()


def sum_and_gather(part, vectors):
    vmem = pl.BlockSpec(memory_space=pltpu.VMEM)
    return pl.pallas_call(
        sum_kernel,
        out_shape=(
            jax.ShapeDtypeStruct((NY, NX, NC, PADDED, 8, 128), F32),
            jax.ShapeDtypeStruct((NY,) + vectors.shape, vectors.dtype),
        ),
        in_specs=[vmem] * 2,
        out_specs=(vmem, vmem),
        scratch_shapes=[
            pltpu.VMEM((NX, PADDED, 8, 128), F32),
            pltpu.VMEM((NX, PADDED, 8, 128), F32),
            pltpu.VMEM((NX - 1, PADDED, 8, 128), F32),
            pltpu.VMEM((PADDED, 8, 128), F32),
            pltpu.VMEM((NZ - 1, PER_Z, 8, 128), F32),
            pltpu.SemaphoreType.DMA((38,)),
            pltpu.SemaphoreType.DMA((38,)),
            pltpu.SemaphoreType.DMA((NY - 1,)),
            pltpu.SemaphoreType.DMA((NY - 1,)),
        ],
        compiler_params=pltpu.CompilerParams(
            collective_id=1, has_side_effects=True, vmem_limit_bytes=40 * 2**20
        ),
        name="sum_and_gather",
    )(part, vectors)


def split(value):
    high = value.astype(BF16)
    return high, (value - high.astype(F32)).astype(BF16)


NT = (((1,), (1,)), ((), ()))
NN = (((1,), (0,)), ((), ()))


def product(a_high, a_low, b_high, b_low, dims):
    def dot(a, b):
        return lax.dot_general(a, b, dims, preferred_element_type=F32)

    return dot(a_high, b_high) + (dot(a_high, b_low) + dot(a_low, b_high))


def newton_kernel(
    full, vectors_ref, codes_ref, rotation_ref, sums_ref,
    whole, a_high, a_low, h, h_high, h_low, t_high, t_low, weights,
):
    y = lax.axis_index("dim")
    rows = vectors_ref.shape[1]

    square = jnp.zeros((8, 128), F32)
    for block in range(NY * NX * NC):
        for t in range(TILES):
            i, j = t // 6, t % 6
            tile = full[block, t]
            square = square + tile * tile
            whole[block * 24 + i * 8 : block * 24 + i * 8 + 8, j * 128 : j * 128 + 128] = tile
    magnitude = jnp.sqrt(jnp.sum(square))
    strips = [pl.ds(s * 256, 256) for s in range(3)]
    for strip in strips:
        a_high[strip], a_low[strip] = split(whole[strip] / magnitude)

    shape = (OWN, D)
    pick = lax.broadcasted_iota(jnp.int32, shape, 0) + y * OWN
    pick = jnp.where(pick == lax.broadcasted_iota(jnp.int32, shape, 1), 1.0, 0.0).astype(BF16)
    own = lax.dot_general(pick, a_high[...], NT, preferred_element_type=F32)
    own = own + lax.dot_general(pick, a_low[...], NT, preferred_element_type=F32)

    for strip in strips:
        value = product(a_high[strip], a_low[strip], a_high[...], a_low[...], NT)
        h[strip] = value
        h_high[strip], h_low[strip] = split(value)

    def times_h(value):
        high, low = split(value)
        return product(high, low, h_high[...], h_low[...], NN)

    for step in range(2):
        own = 1.5 * own - 0.5 * times_h(own)
        for strip in strips:
            value = product(h_high[strip], h_low[strip], h_high[...], h_low[...], NN)
            value = 1.5 * h[strip] - 0.5 * value
            whole[strip] = value
            t_high[strip], t_low[strip] = split(value)
        for strip in strips:
            value = product(t_high[strip], t_low[strip], h_high[...], h_low[...], NN)
            h[strip] = 1.5 * whole[strip] - 0.5 * value
        for strip in strips:
            h_high[strip], h_low[strip] = split(h[strip])
    own = 1.5 * own - 0.5 * times_h(own)
    last = times_h(own)
    for _ in range(2):
        last = 1.5 * last - 0.5 * times_h(last)
    own = 1.5 * own - 0.5 * last
    rotation_ref[...] = own

    rotated = jnp.dot(own.astype(BF16), vectors_ref[...], preferred_element_type=F32)
    rotated = rotated.astype(BF16).astype(F32)
    weights[:, :OWN] = rotated.T.astype(BF16)
    weights[:, OWN:] = jnp.where(
        lax.broadcasted_iota(jnp.int32, (rows, K - OWN), 1) < OWN_M, 1.0, 0.0
    ).astype(BF16)
    level = lax.broadcasted_iota(jnp.int32, (K, rows), 0)
    column = lax.broadcasted_iota(jnp.int32, (K, K), 1)
    subspace = jnp.where(column < OWN, column // SUB, column - OWN)
    total = jnp.zeros((K, K), F32)
    for m in range(OWN_M):
        onehot = jnp.where(level == codes_ref[m : m + 1, :], 1.0, 0.0).astype(BF16)
        value = jnp.dot(onehot, weights[...], preferred_element_type=F32)
        total = jnp.where(subspace == m, value, total)
    sums_ref[...] = total


def newton_and_sums(full, vectors_all, codes):
    rows = codes.shape[1]
    vmem = pl.BlockSpec(memory_space=pltpu.VMEM)
    square = (D, D)
    return pl.pallas_call(
        newton_kernel,
        out_shape=(
            jax.ShapeDtypeStruct((OWN, D), F32),
            jax.ShapeDtypeStruct((K, K), F32),
        ),
        in_specs=[vmem] * 3,
        out_specs=(vmem, vmem),
        scratch_shapes=[pltpu.VMEM(square, F32)]
        + [pltpu.VMEM(square, BF16)] * 2
        + [pltpu.VMEM(square, F32)]
        + [pltpu.VMEM(square, BF16)] * 4
        + [pltpu.VMEM((rows, K), BF16)],
        compiler_params=pltpu.CompilerParams(vmem_limit_bytes=50 * 2**20),
        name="newton_and_sums",
    )(full, vectors_all, codes)


def refit_kernel(sums_ref, book_ref, box_x, sum_x, box_z, mine, box_core, send_sem, recv_sem):
    x, z, core, y = position()
    sibling = device(x, z, 1 - core, y)
    across_x = [device(lax.rem(x + off, NX), z, core, y) for off in range(1, NX)]
    across_z = [device(x, lax.rem(z + off, NZ), core, y) for off in range(1, NZ)]
    greet([sibling] + across_x + across_z)
    sent = []

    def send(src, dst, k, peer):
        copy = remote(src, dst, send_sem, recv_sem, k, peer)
        copy.start()
        sent.append(copy)
        return copy

    stage = [
        send(sums_ref.at[lax.rem(x + i + 1, NX)], box_x.at[i], i, peer)
        for i, peer in enumerate(across_x)
    ]
    for copy in stage:
        copy.wait_recv()
    sum_x[...] = (sums_ref[x] + box_x[0]) + (box_x[1] + box_x[2])
    stage = [
        send(sum_x.at[lax.rem(z + i + 1, NZ)], box_z.at[i], 3 + i, peer)
        for i, peer in enumerate(across_z)
    ]
    for copy in stage:
        copy.wait_recv()
    total = sum_x[z]
    for i in range(NZ - 1):
        total = total + box_z[i]
    mine[...] = total
    send(mine, box_core, 10, sibling).wait_recv()
    book_ref[...] = mine[...] + box_core[...]
    for copy in sent:
        copy.wait_send()


def refit(sums):
    vmem = pl.BlockSpec(memory_space=pltpu.VMEM)
    return pl.pallas_call(
        refit_kernel,
        out_shape=jax.ShapeDtypeStruct((8, K), F32),
        in_specs=[vmem],
        out_specs=vmem,
        scratch_shapes=[
            pltpu.VMEM((NX - 1, NZ, 8, K), F32),
            pltpu.VMEM((NZ, 8, K), F32),
            pltpu.VMEM((NZ - 1, 8, K), F32),
            pltpu.VMEM((8, K), F32),
            pltpu.VMEM((8, K), F32),
            pltpu.SemaphoreType.DMA((11,)),
            pltpu.SemaphoreType.DMA((11,)),
        ],
        compiler_params=pltpu.CompilerParams(collective_id=2, has_side_effects=True),
        name="refit",
    )(sums)


def per_device(vectors, codes, codebook):
    rows = vectors.shape[1]
    codes_all, book_all = gather_codes(codes.astype(BF16), codebook.T)
    part = cross_part(codes_all.reshape(M, rows), book_all.reshape(D, K), vectors)
    full, vectors_all = sum_and_gather(
        part.reshape(NX, NC, PADDED, 8, 128), vectors
    )
    rotation, sums = newton_and_sums(
        full.reshape(NY * NX * NC, PADDED, 8, 128), vectors_all.reshape(D, rows), codes
    )
    pair = refit(sums.reshape(NX, NZ, 8, K))
    core = lax.rem(lax.axis_index("dp"), NC)
    mine = lax.dynamic_slice_in_dim(pair, core * (K // (NX * NZ * NC)), K // (NX * NZ * NC), 0)
    divisor = jnp.repeat(jnp.maximum(mine[:, OWN : OWN + OWN_M], 1.0), SUB, axis=1)
    return (rotation, mine[:, :OWN] / divisor)


def solution(mesh):
    placed = (P("dim", "dp"), P("dim", "dp"), P(None, "dim"))
    return jax.shard_map(
        per_device,
        mesh=mesh,
        in_specs=placed,
        out_specs=(P("dim", None), P("dp", "dim")),
        check_vma=False,
    )
```

```python
import jax
import jax.numpy as jnp
from jax import lax
from jax.experimental import pallas as pl
from jax.experimental.pallas import tpu as pltpu
from jax.sharding import PartitionSpec as P

NX, NZ, NC, NY = 4, 8, 2, 4
D, M, K = 768, 64, 256
SUB = D // M
OWN = D // NY
OWN_M = M // NY
TILES = 18
PER_Z = 3
HALF = TILES // 2
ROWS_K = K // NX // NC
MESH = pl.DeviceIdType.MESH
F32, BF16 = jnp.float32, jnp.bfloat16
NT = (((1,), (1,)), ((), ()))
NN = (((1,), (0,)), ((), ()))


def dot(a, b, dims):
    return lax.dot_general(a, b, dims, preferred_element_type=F32)


def split(value):
    high = value.astype(BF16)
    return high, (value - high.astype(F32)).astype(BF16)


def product(a_high, a_low, b_high, b_low, dims):
    return dot(a_high, b_high, dims) + (dot(a_high, b_low, dims) + dot(a_low, b_high, dims))


def position():
    dp = lax.axis_index("dp")
    y = lax.axis_index("dim")
    core = lax.rem(dp, NC)
    z = lax.rem(dp // NC, NZ)
    x = dp // (NC * NZ)
    return x, z, core, y


def device(x, z, core, y):
    return ((x * NZ + z) * NC + core, y)


def own_rows(y):
    return pl.ds(pl.multiple_of(y * OWN, 64), OWN)


def decode(codes_all, book_all, decoded, y):
    group = OWN_M // 2
    height = group * SUB
    rows = decoded.shape[1]
    which = lax.broadcasted_iota(jnp.int32, (height, 128), 0) // SUB
    for g in range(2):
        book = book_all[y, g * height : (g + 1) * height, :].astype(F32)
        low, high = book[:, :128], book[:, 128:]
        base = pl.multiple_of(y * OWN + g * height, 32)
        for block in range(rows // 128):
            cols = pl.ds(block * 128, 128)
            lines = codes_all[y, :, cols].astype(F32).astype(jnp.int32)
            index = jnp.broadcast_to(lines[g * group : g * group + 1], (height, 128))
            for s in range(1, group):
                line = lines[g * group + s : g * group + s + 1]
                index = jnp.where(which == s, jnp.broadcast_to(line, (height, 128)), index)
            lane = index & 127
            picked = jnp.where(
                index >= 128,
                jnp.take_along_axis(high, lane, axis=1),
                jnp.take_along_axis(low, lane, axis=1),
            )
            decoded[pl.ds(base, height), cols] = picked.astype(BF16)


def newton(y, whole, a_high, a_low, h, h_high, h_low, t_high, t_low):
    square = jnp.zeros((8, 128), F32)
    for s in range(D // 8):
        for j in range(D // 128):
            tile = whole[s * 8 : s * 8 + 8, j * 128 : j * 128 + 128]
            square = square + tile * tile
    energy = jnp.sum(square)
    side = 256
    count = D // side

    def cut(i):
        return slice(i * side, i * side + side)

    for i in range(count):
        a_high[cut(i)], a_low[cut(i)] = split(whole[cut(i)])

    shape = (OWN, D)
    pick = lax.broadcasted_iota(jnp.int32, shape, 0) + y * OWN
    pick = jnp.where(pick == lax.broadcasted_iota(jnp.int32, shape, 1), 1.0, 0.0).astype(BF16)
    own = dot(pick, a_high[...], NT) + dot(pick, a_low[...], NT)
    own = own / jnp.sqrt(energy)

    upper = [(i, j) for i in range(count) for j in range(i, count)]

    def put(full, high, low, i, j, value):
        full[cut(i), cut(j)] = value
        high[cut(i), cut(j)], low[cut(i), cut(j)] = split(value)
        if i != j:
            high[cut(j), cut(i)], low[cut(j), cut(i)] = split(value.T)

    def times_h(value):
        high, low = split(value)
        return product(high, low, h_high[...], h_low[...], NN)

    for i, j in upper:
        value = product(a_high[cut(i)], a_low[cut(i)], a_high[cut(j)], a_low[cut(j)], NT)
        put(h, h_high, h_low, i, j, value / energy)
    for step in range(2):
        own = 1.5 * own - 0.5 * times_h(own)
        for i, j in upper:
            value = product(h_high[cut(i)], h_low[cut(i)], h_high[:, cut(j)], h_low[:, cut(j)], NN)
            put(whole, t_high, t_low, i, j, 1.5 * h[cut(i), cut(j)] - 0.5 * value)
        for i, j in upper:
            value = product(t_high[cut(i)], t_low[cut(i)], h_high[:, cut(j)], h_low[:, cut(j)], NN)
            h[cut(i), cut(j)] = 1.5 * whole[cut(i), cut(j)] - 0.5 * value
        for i, j in upper:
            put(h, h_high, h_low, i, j, h[cut(i), cut(j)])
    own = 1.5 * own - 0.5 * times_h(own)
    last = times_h(own)
    for _ in range(2):
        last = 1.5 * last - 0.5 * times_h(last)
    return 1.5 * own - 0.5 * last


def kernel(
    vectors_ref, codes_ref, book_ref, rotation_ref, refit_ref,
    codes_all, book_all, vectors_all, decoded, part, box_core, sum_core, box_x, sum_x, box_z,
    full, whole, a_high, a_low, h, h_high, h_low, t_high, t_low,
    onehot, weights, sums, box_one, stage_two, box_two, send_sem, recv_sem,
):
    x, z, core, y = position()
    rows = vectors_ref.shape[1]
    sibling = device(x, z, 1 - core, y)
    across_x = [device(lax.rem(x + off, NX), z, core, y) for off in range(1, NX)]
    across_z = [device(x, lax.rem(z + off, NZ), core, y) for off in range(1, NZ)]
    across_y = [device(x, z, core, lax.rem(y + off, NY)) for off in range(1, NY)]
    other_x = [
        device(lax.rem(x + off, NX), z, 1 - core, y) for off in range(1, NX)
    ]
    sent = []
    number = [0]

    def send(src, dst, peer):
        k = number[0]
        number[0] += 1
        copy = pltpu.make_async_remote_copy(
            src_ref=src, dst_ref=dst, send_sem=send_sem.at[k], recv_sem=recv_sem.at[k],
            device_id=peer, device_id_type=MESH,
        )
        copy.start()
        sent.append(copy)
        return copy

    def spread(ref, peers):
        return [send(ref, ref, peer) for peer in peers]

    barrier = pltpu.get_barrier_semaphore()
    peers = [sibling] + across_x + other_x + across_z + across_y
    for peer in peers:
        pl.semaphore_signal(barrier, inc=1, device_id=peer, device_id_type=MESH)
    codes_all[y] = codes_ref[...].astype(F32).astype(BF16)
    book_all[y] = book_ref[...]
    sum_x[TILES:] = jnp.zeros((PER_Z * NZ - TILES, 8, 128), F32)
    stage_two[...] = jnp.zeros((NZ, 8, K), F32)
    weights[OWN:, :] = jnp.where(
        lax.broadcasted_iota(jnp.int32, (K - OWN, rows), 0) < OWN_M, 1.0, 0.0
    ).astype(BF16)
    pl.semaphore_wait(barrier, len(peers))

    arrivals = []
    for peer in across_y:
        arrivals.append(spread(codes_all.at[y], [peer]) + spread(book_all.at[y], [peer]))
    vectors_all[own_rows(y), :] = vectors_ref[...]
    decode(codes_all, book_all, decoded, y)
    for i, copies in enumerate(arrivals):
        for copy in copies:
            copy.wait_recv()
        decode(codes_all, book_all, decoded, lax.rem(y + NY - 1 - i, NY))
    mine = vectors_all.at[own_rows(y), :]
    vectors_here = spread(mine, across_y)

    value = dot(vectors_ref[...], decoded[...], NT)
    for pair in range(NX * NC):
        for t in range(TILES):
            i, j = pair * 3 + t // 6, t % 6
            part[pair // NC, pair % NC, t] = value[i * 8 : i * 8 + 8, j * 128 : j * 128 + 128]

    order = [lax.rem(x + off, NX) for off in (1, 2, 3, 0)]
    first = [send(part.at[i, 1 - core], box_core.at[i], sibling) for i in order]
    stage = []
    for n, copy in enumerate(first):
        i = order[n]
        copy.wait_recv()
        sum_core[i] = part[i, core] + box_core[i]
        if n < NX - 1:
            stage.append(send(sum_core.at[i], box_x.at[n], across_x[n]))
    place = lax.broadcasted_iota(jnp.int32, (K, rows), 0)
    level = ((place // 64) * 16 + (place // 4) % NZ * 2 + (place // 32) % NC) * 4 + place % 4
    for m in range(OWN_M):
        onehot[m * K : m * K + K] = jnp.where(level == codes_ref[m : m + 1, :], 1.0, 0.0).astype(BF16)
    for copy in stage:
        copy.wait_recv()
    sum_x[:TILES] = (sum_core[x] + box_x[0]) + (box_x[1] + box_x[2])
    stage = [
        send(sum_x.at[pl.ds(lax.rem(z + i + 1, NZ) * PER_Z, PER_Z)], box_z.at[i], peer)
        for i, peer in enumerate(across_z)
    ]
    for copy in stage:
        copy.wait_recv()
    share = pl.ds(z * PER_Z, PER_Z)
    total = sum_x[share]
    for i in range(NZ - 1):
        total = total + box_z[i]
    full[y, x, core, share] = total

    for copy in spread(full.at[y, x, core, share], across_z):
        copy.wait_recv()

    def piece(y, x, core, half):
        return full.at[y, x, core, pl.ds(half * HALF, HALF)]

    def lay(y, x, core, half):
        base = ((y * NX + x) * NC + core) * 24
        for t in range(half * HALF, half * HALF + HALF):
            row = pl.multiple_of(base + t // 6 * 8, 8)
            col = t % 6 * 128
            whole[pl.ds(row, 8), col : col + 128] = full[y, x, core, t]

    def before(index, off, size):
        return lax.rem(index + size - off, size)

    one, two = piece(y, x, core, 0), piece(y, x, core, 1)
    one_x, two_y = spread(one, across_x), spread(two, across_y)
    one_y, two_x = [spread(one, across_y)], [spread(two, across_x)]
    siblings = [(spread(one, [sibling])[0], y, x, 0), (spread(two, [sibling])[0], y, x, 1)]
    lay(y, x, core, 0)
    lay(y, x, core, 1)
    for i in range(NX - 1):
        from_x = before(x, i + 1, NX)
        one_x[i].wait_recv()
        ref = piece(y, from_x, core, 0)
        one_y.append(spread(ref, across_y))
        siblings.append((spread(ref, [sibling])[0], y, from_x, 0))
        from_y = before(y, i + 1, NY)
        two_y[i].wait_recv()
        ref = piece(from_y, x, core, 1)
        two_x.append(spread(ref, across_x))
        siblings.append((spread(ref, [sibling])[0], from_y, x, 1))
        lay(y, from_x, core, 0)
        lay(from_y, x, core, 1)
    for n in range(NX):
        for i in range(NX - 1):
            at_x, at_y = before(x, n, NX), before(y, i + 1, NY)
            one_y[n][i].wait_recv()
            siblings.append((spread(piece(at_y, at_x, core, 0), [sibling])[0], at_y, at_x, 0))
            lay(at_y, at_x, core, 0)
            at_x, at_y = before(x, i + 1, NX), before(y, n, NY)
            two_x[n][i].wait_recv()
            siblings.append((spread(piece(at_y, at_x, core, 1), [sibling])[0], at_y, at_x, 1))
            lay(at_y, at_x, core, 1)
    for copy, at_y, at_x, half in siblings:
        copy.wait_recv()
        lay(at_y, at_x, 1 - core, half)

    rotation = newton(y, whole, a_high, a_low, h, h_high, h_low, t_high, t_low)
    rotation_ref[...] = rotation

    for copy in vectors_here:
        copy.wait_recv()
    rotated = dot(rotation.astype(BF16), vectors_all[...], NN)
    weights[:OWN, :] = rotated.astype(BF16)
    column = lax.broadcasted_iota(jnp.int32, (K, K), 1)
    subspace = jnp.where(column < OWN, column // SUB, column - OWN)
    total = jnp.zeros((K, K), F32)
    for m in range(OWN_M):
        value = dot(onehot[m * K : m * K + K], weights[...], NT)
        total = jnp.where(subspace == m, value, total)
    for i in range(NX * NC):
        sums[i] = total[i * ROWS_K : (i + 1) * ROWS_K]

    stage = []
    for peers, core_to in ((across_x, core), ([sibling] + other_x, 1 - core)):
        for i, peer in enumerate(peers):
            off = i + 1 if len(peers) == NX - 1 else i
            target = lax.rem(x + off, NX) * NC + core_to
            stage.append(send(sums.at[target], box_one.at[len(stage)], peer))
    for copy in stage:
        copy.wait_recv()
    total = sums[x * NC + core]
    for i in range(len(stage)):
        total = total + box_one[i]
    for i in range(NZ):
        stage_two[i, 0:4] = total[i * 4 : i * 4 + 4]
    stage = [
        send(stage_two.at[lax.rem(z + i + 1, NZ)], box_two.at[i], peer)
        for i, peer in enumerate(across_z)
    ]
    for copy in stage:
        copy.wait_recv()
    total = stage_two[z]
    for i in range(NZ - 1):
        total = total + box_two[i]
    left, right = total[:, :128], total[:, 128:]
    lane = lax.broadcasted_iota(jnp.int32, (8, 128), 1)
    offset = OWN - 128
    count = jnp.take_along_axis(right, offset + lane // SUB, axis=1)
    refit_ref[:, :128] = (left / jnp.maximum(count, 1.0))[0:4]
    count = jnp.take_along_axis(right, offset + jnp.minimum((lane + 128) // SUB, OWN_M - 1), axis=1)
    refit_ref[:, 128:] = (right / jnp.maximum(count, 1.0))[0:4, :offset]
    for copy in sent:
        copy.wait_send()


def per_device(vectors, codes, codebook):
    rows = vectors.shape[1]
    vmem = pl.BlockSpec(memory_space=pltpu.VMEM)
    square = (D, D)
    copies = 6 + 3 + 4 + 3 + 7 + 7 + 12 + 2 + 24 + 24 + 7 + 7
    rotation, refit = pl.pallas_call(
        kernel,
        out_shape=(
            jax.ShapeDtypeStruct((OWN, D), F32),
            jax.ShapeDtypeStruct((K // (NX * NZ * NC), OWN), F32),
        ),
        in_specs=[vmem] * 3,
        out_specs=(vmem, vmem),
        scratch_shapes=[
            pltpu.VMEM((NY, OWN_M, rows), BF16),
            pltpu.VMEM((NY, OWN, K), BF16),
            pltpu.VMEM((D, rows), BF16),
            pltpu.VMEM((D, rows), BF16),
            pltpu.VMEM((NX, NC, TILES, 8, 128), F32),
            pltpu.VMEM((NX, TILES, 8, 128), F32),
            pltpu.VMEM((NX, TILES, 8, 128), F32),
            pltpu.VMEM((NX - 1, TILES, 8, 128), F32),
            pltpu.VMEM((PER_Z * NZ, 8, 128), F32),
            pltpu.VMEM((NZ - 1, PER_Z, 8, 128), F32),
            pltpu.VMEM((NY, NX, NC, PER_Z * NZ, 8, 128), F32),
            pltpu.VMEM(square, F32),
            pltpu.VMEM(square, BF16),
            pltpu.VMEM(square, BF16),
            pltpu.VMEM(square, F32),
            pltpu.VMEM(square, BF16),
            pltpu.VMEM(square, BF16),
            pltpu.VMEM(square, BF16),
            pltpu.VMEM(square, BF16),
            pltpu.VMEM((OWN_M * K, rows), BF16),
            pltpu.VMEM((K, rows), BF16),
            pltpu.VMEM((NX * NC, ROWS_K, K), F32),
            pltpu.VMEM((NX * NC - 1, ROWS_K, K), F32),
            pltpu.VMEM((NZ, 8, K), F32),
            pltpu.VMEM((NZ - 1, 8, K), F32),
            pltpu.SemaphoreType.DMA((copies,)),
            pltpu.SemaphoreType.DMA((copies,)),
        ],
        compiler_params=pltpu.CompilerParams(
            collective_id=0, has_side_effects=True, vmem_limit_bytes=56 * 2**20
        ),
        name="rotate_and_refit",
    )(vectors, codes, codebook.T)
    return rotation, refit


def solution(mesh):
    placed = (P("dim", "dp"), P("dim", "dp"), P(None, "dim"))
    return jax.shard_map(
        per_device,
        mesh=mesh,
        in_specs=placed,
        out_specs=(P("dim", None), P("dp", "dim")),
        check_vma=False,
    )
```

```python
import jax
import jax.numpy as jnp
from jax import lax
from jax.experimental import pallas as pl
from jax.experimental.pallas import tpu as pltpu
from jax.sharding import PartitionSpec as P

NX, NZ, NC, NY = 4, 8, 2, 4
D, M, K = 768, 64, 256
SUB = D // M
OWN = D // NY
OWN_M = M // NY
TILES = 18
PER_Z = 3
HALF = TILES // 2
ROWS_K = K // NX // NC
MESH = pl.DeviceIdType.MESH
F32, BF16 = jnp.float32, jnp.bfloat16
NT = (((1,), (1,)), ((), ()))
NN = (((1,), (0,)), ((), ()))


def dot(a, b, dims):
    return lax.dot_general(a, b, dims, preferred_element_type=F32)


def split(value):
    high = value.astype(BF16)
    return high, (value - high.astype(F32)).astype(BF16)


def product(a_high, a_low, b_high, b_low, dims):
    return dot(a_high, b_high, dims) + (dot(a_high, b_low, dims) + dot(a_low, b_high, dims))


def position():
    dp = lax.axis_index("dp")
    y = lax.axis_index("dim")
    core = lax.rem(dp, NC)
    z = lax.rem(dp // NC, NZ)
    x = dp // (NC * NZ)
    return x, z, core, y


def device(x, z, core, y):
    return ((x * NZ + z) * NC + core, y)


def own_rows(y):
    return pl.ds(pl.multiple_of(y * OWN, 64), OWN)


def decode(codes_all, book_all, decoded, y):
    group = OWN_M // 2
    height = group * SUB
    rows = decoded.shape[1]
    which = lax.broadcasted_iota(jnp.int32, (height, 128), 0) // SUB
    for g in range(2):
        book = book_all[y, g * height : (g + 1) * height, :].astype(F32)
        low, high = book[:, :128], book[:, 128:]
        base = pl.multiple_of(y * OWN + g * height, 32)
        for block in range(rows // 128):
            cols = pl.ds(block * 128, 128)
            lines = codes_all[y, :, cols].astype(F32).astype(jnp.int32)
            index = jnp.broadcast_to(lines[g * group : g * group + 1], (height, 128))
            for s in range(1, group):
                line = lines[g * group + s : g * group + s + 1]
                index = jnp.where(which == s, jnp.broadcast_to(line, (height, 128)), index)
            lane = index & 127
            picked = jnp.where(
                index >= 128,
                jnp.take_along_axis(high, lane, axis=1),
                jnp.take_along_axis(low, lane, axis=1),
            )
            decoded[pl.ds(base, height), cols] = picked.astype(BF16)


def newton(y, whole, a_high, a_low, h, h_high, h_low, t_high, t_low):
    squares = [jnp.zeros((8, 128), F32)] * 12
    for s in range(D // 8):
        for j in range(D // 128):
            tile = whole[s * 8 : s * 8 + 8, j * 128 : j * 128 + 128]
            n = s % 2 * 6 + j
            squares[n] = squares[n] + tile * tile
    energy = jnp.sum(sum(squares[1:], squares[0]))
    scale = 1.0 / energy
    side = 256
    count = D // side

    def cut(i):
        return slice(i * side, i * side + side)

    for i in range(count):
        a_high[cut(i)], a_low[cut(i)] = split(whole[cut(i)])

    start = pl.multiple_of(y * OWN - 64 * lax.rem(y, 2), 128)
    own = whole[:, pl.ds(start, 256)]
    own = jnp.where(lax.rem(y, 2) == 1, pltpu.roll(own, 192, 1), own)
    own = own.T[:OWN] / jnp.sqrt(energy)

    upper = [(i, j) for i in range(count) for j in range(i, count)]

    def put(full, high, low, i, j, value):
        full[cut(i), cut(j)] = value
        high[cut(i), cut(j)], low[cut(i), cut(j)] = split(value)
        if i != j:
            high[cut(j), cut(i)], low[cut(j), cut(i)] = split(value.T)

    def times_h(value):
        high, low = split(value)
        return product(high, low, h_high[...], h_low[...], NN)

    for i, j in upper:
        value = product(a_high[cut(i)], a_low[cut(i)], a_high[cut(j)], a_low[cut(j)], NT)
        put(h, h_high, h_low, i, j, value * scale)
    for step in range(2):
        own = 1.5 * own - 0.5 * times_h(own)
        for i, j in upper:
            value = product(h_high[cut(i)], h_low[cut(i)], h_high[:, cut(j)], h_low[:, cut(j)], NN)
            put(whole, t_high, t_low, i, j, 1.5 * h[cut(i), cut(j)] - 0.5 * value)
        for i, j in upper:
            value = product(t_high[cut(i)], t_low[cut(i)], h_high[:, cut(j)], h_low[:, cut(j)], NN)
            h[cut(i), cut(j)] = 1.5 * whole[cut(i), cut(j)] - 0.5 * value
        for i, j in upper:
            put(h, h_high, h_low, i, j, h[cut(i), cut(j)])
    own = 1.5 * own - 0.5 * times_h(own)
    last = times_h(own)
    for _ in range(2):
        last = 1.5 * last - 0.5 * times_h(last)
    return 1.5 * own - 0.5 * last


def kernel(
    vectors_hbm, codes_hbm, book_hbm, rotation_hbm, refit_ref,
    codes_ref, rotation_ref, codes_all, book_all, vectors_all, decoded, part, box_core, sum_core, box_x, sum_x, box_z,
    full, whole, a_high, a_low, h, h_high, h_low, t_high, t_low,
    onehot, weights, sums, box_one, stage_two, box_two, send_sem, recv_sem, local_sem,
):
    x, z, core, y = position()
    rows = vectors_all.shape[1]
    sibling = device(x, z, 1 - core, y)
    across_x = [device(lax.rem(x + off, NX), z, core, y) for off in range(1, NX)]
    across_z = [device(x, lax.rem(z + off, NZ), core, y) for off in range(1, NZ)]
    across_y = [device(x, z, core, lax.rem(y + off, NY)) for off in range(1, NY)]
    other_x = [
        device(lax.rem(x + off, NX), z, 1 - core, y) for off in range(1, NX)
    ]
    sent = []
    number = [0]

    def send(src, dst, peer):
        k = number[0]
        number[0] += 1
        copy = pltpu.make_async_remote_copy(
            src_ref=src, dst_ref=dst, send_sem=send_sem.at[k], recv_sem=recv_sem.at[k],
            device_id=peer, device_id_type=MESH,
        )
        copy.start()
        sent.append(copy)
        return copy

    def spread(ref, peers):
        return [send(ref, ref, peer) for peer in peers]

    barrier = pltpu.get_barrier_semaphore()
    peers = [sibling] + across_x + other_x + across_z + across_y
    for peer in peers:
        pl.semaphore_signal(barrier, inc=1, device_id=peer, device_id_type=MESH)
    mine = vectors_all.at[own_rows(y), :]
    load_codes = pltpu.make_async_copy(codes_hbm, codes_ref, local_sem.at[0])
    load_book = pltpu.make_async_copy(book_hbm, book_all.at[y], local_sem.at[1])
    load_vectors = pltpu.make_async_copy(vectors_hbm, mine, local_sem.at[2])
    for copy in (load_codes, load_book, load_vectors):
        copy.start()
    sum_x[TILES:] = jnp.zeros((PER_Z * NZ - TILES, 8, 128), F32)
    stage_two[...] = jnp.zeros((NZ, 8, K), F32)
    weights[OWN:, :] = jnp.where(
        lax.broadcasted_iota(jnp.int32, (K - OWN, rows), 0) < OWN_M, 1.0, 0.0
    ).astype(BF16)
    load_codes.wait()
    codes_all[y] = codes_ref[...].astype(F32).astype(BF16)
    load_book.wait()
    load_vectors.wait()
    pl.semaphore_wait(barrier, len(peers))

    arrivals = []
    for peer in across_y:
        arrivals.append(spread(codes_all.at[y], [peer]) + spread(book_all.at[y], [peer]))
    decode(codes_all, book_all, decoded, y)
    for i, copies in enumerate(arrivals):
        for copy in copies:
            copy.wait_recv()
        decode(codes_all, book_all, decoded, lax.rem(y + NY - 1 - i, NY))
    vectors_here = spread(mine, across_y)

    value = dot(vectors_all[own_rows(y), :], decoded[...], NT)
    for pair in range(NX * NC):
        for t in range(TILES):
            i, j = pair * 3 + t // 6, t % 6
            part[pair // NC, pair % NC, t] = value[i * 8 : i * 8 + 8, j * 128 : j * 128 + 128]

    order = [lax.rem(x + off, NX) for off in (1, 2, 3, 0)]
    first = [send(part.at[i, 1 - core], box_core.at[i], sibling) for i in order]
    stage = []
    for n, copy in enumerate(first):
        i = order[n]
        copy.wait_recv()
        sum_core[i] = part[i, core] + box_core[i]
        if n < NX - 1:
            stage.append(send(sum_core.at[i], box_x.at[n], across_x[n]))
    place = lax.broadcasted_iota(jnp.int32, (ROWS_K, rows), 0)
    level = place // 4 * 8 + place % 4
    for m in range(OWN_M):
        code = jnp.broadcast_to(codes_ref[m : m + 1, :], (ROWS_K, rows))
        for chunk in range(NX * NC):
            at = (chunk * OWN_M + m) * ROWS_K
            same = level == code - (chunk // NC * 64 + chunk % NC * 4)
            onehot[at : at + ROWS_K] = jnp.where(same, 1.0, 0.0).astype(BF16)
    for copy in stage:
        copy.wait_recv()
    sum_x[:TILES] = (sum_core[x] + box_x[0]) + (box_x[1] + box_x[2])
    stage = [
        send(sum_x.at[pl.ds(lax.rem(z + i + 1, NZ) * PER_Z, PER_Z)], box_z.at[i], peer)
        for i, peer in enumerate(across_z)
    ]
    for copy in stage:
        copy.wait_recv()
    share = pl.ds(z * PER_Z, PER_Z)
    total = sum_x[share]
    for i in range(NZ - 1):
        total = total + box_z[i]
    full[y, x, core, share] = total

    for copy in spread(full.at[y, x, core, share], across_z):
        copy.wait_recv()

    def piece(y, x, core, half):
        return full.at[y, x, core, pl.ds(half * HALF, HALF)]

    def lay(y, x, core, half):
        base = ((y * NX + x) * NC + core) * 24
        for t in range(half * HALF, half * HALF + HALF):
            row = pl.multiple_of(base + t // 6 * 8, 8)
            col = t % 6 * 128
            whole[pl.ds(row, 8), col : col + 128] = full[y, x, core, t]

    def before(index, off, size):
        return lax.rem(index + size - off, size)

    one, two = piece(y, x, core, 0), piece(y, x, core, 1)
    one_x, two_y = spread(one, across_x), spread(two, across_y)
    one_y, two_x = [spread(one, across_y)], [spread(two, across_x)]
    siblings = [(spread(one, [sibling])[0], y, x, 0), (spread(two, [sibling])[0], y, x, 1)]
    lay(y, x, core, 0)
    lay(y, x, core, 1)
    for i in range(NX - 1):
        from_x = before(x, i + 1, NX)
        one_x[i].wait_recv()
        ref = piece(y, from_x, core, 0)
        one_y.append(spread(ref, across_y))
        siblings.append((spread(ref, [sibling])[0], y, from_x, 0))
        from_y = before(y, i + 1, NY)
        two_y[i].wait_recv()
        ref = piece(from_y, x, core, 1)
        two_x.append(spread(ref, across_x))
        siblings.append((spread(ref, [sibling])[0], from_y, x, 1))
        lay(y, from_x, core, 0)
        lay(from_y, x, core, 1)
    for n in range(NX):
        for i in range(NX - 1):
            at_x, at_y = before(x, n, NX), before(y, i + 1, NY)
            one_y[n][i].wait_recv()
            siblings.append((spread(piece(at_y, at_x, core, 0), [sibling])[0], at_y, at_x, 0))
            lay(at_y, at_x, core, 0)
            at_x, at_y = before(x, i + 1, NX), before(y, n, NY)
            two_x[n][i].wait_recv()
            siblings.append((spread(piece(at_y, at_x, core, 1), [sibling])[0], at_y, at_x, 1))
            lay(at_y, at_x, core, 1)
    for copy, at_y, at_x, half in siblings:
        copy.wait_recv()
        lay(at_y, at_x, 1 - core, half)

    rotation = newton(y, whole, a_high, a_low, h, h_high, h_low, t_high, t_low)
    rotation_ref[...] = rotation
    store_rotation = pltpu.make_async_copy(rotation_ref, rotation_hbm, local_sem.at[3])
    store_rotation.start()

    for copy in vectors_here:
        copy.wait_recv()
    rotated = dot(rotation.astype(BF16), vectors_all[...], NN)
    weights[:OWN, :] = rotated.astype(BF16)
    column = lax.broadcasted_iota(jnp.int32, (ROWS_K, K), 1)
    subspace = jnp.where(column < OWN, column // SUB, column - OWN)

    stage = []
    height = OWN_M * ROWS_K
    for n, (off, flip) in enumerate(((2, 0), (2, 1), (1, 0), (1, 1), (3, 0), (3, 1), (0, 1), (0, 0))):
        to_x, to_core = lax.rem(x + off, NX), lax.rem(core + flip, NC)
        chunk = pl.multiple_of((to_x * NC + to_core) * height, height)
        value = dot(onehot[pl.ds(chunk, height)], weights[...], NT)
        total = jnp.zeros((ROWS_K, K), F32)
        for m in range(OWN_M):
            total = jnp.where(subspace == m, value[m * ROWS_K : (m + 1) * ROWS_K], total)
        sums[n] = total
        if n < NX * NC - 1:
            stage.append(send(sums.at[n], box_one.at[n], device(to_x, z, to_core, y)))
    for copy in stage:
        copy.wait_recv()
    total = sums[NX * NC - 1]
    for i in range(len(stage)):
        total = total + box_one[i]
    for i in range(NZ):
        stage_two[i, 0:4] = total[i * 4 : i * 4 + 4]
    stage = [
        send(stage_two.at[lax.rem(z + i + 1, NZ)], box_two.at[i], peer)
        for i, peer in enumerate(across_z)
    ]
    for copy in stage:
        copy.wait_recv()
    total = stage_two[z]
    for i in range(NZ - 1):
        total = total + box_two[i]
    left, right = total[:, :128], total[:, 128:]
    lane = lax.broadcasted_iota(jnp.int32, (8, 128), 1)
    offset = OWN - 128
    count = jnp.take_along_axis(right, offset + lane // SUB, axis=1)
    refit_ref[:, :128] = (left / jnp.maximum(count, 1.0))[0:4]
    count = jnp.take_along_axis(right, offset + jnp.minimum((lane + 128) // SUB, OWN_M - 1), axis=1)
    refit_ref[:, 128:] = (right / jnp.maximum(count, 1.0))[0:4, :offset]
    for copy in sent:
        copy.wait_send()
    store_rotation.wait()


def per_device(vectors, codes, codebook):
    rows = vectors.shape[1]
    vmem = pl.BlockSpec(memory_space=pltpu.VMEM)
    anywhere = pl.BlockSpec(memory_space=pl.ANY)
    square = (D, D)
    copies = 6 + 3 + 4 + 3 + 7 + 7 + 12 + 2 + 24 + 24 + 7 + 7
    rotation, refit = pl.pallas_call(
        kernel,
        out_shape=(
            jax.ShapeDtypeStruct((OWN, D), F32),
            jax.ShapeDtypeStruct((K // (NX * NZ * NC), OWN), F32),
        ),
        in_specs=[anywhere] * 3,
        out_specs=(anywhere, vmem),
        scratch_shapes=[
            pltpu.VMEM((OWN_M, rows), jnp.int32),
            pltpu.VMEM((OWN, D), F32),
            pltpu.VMEM((NY, OWN_M, rows), BF16),
            pltpu.VMEM((NY, OWN, K), BF16),
            pltpu.VMEM((D, rows), BF16),
            pltpu.VMEM((D, rows), BF16),
            pltpu.VMEM((NX, NC, TILES, 8, 128), F32),
            pltpu.VMEM((NX, TILES, 8, 128), F32),
            pltpu.VMEM((NX, TILES, 8, 128), F32),
            pltpu.VMEM((NX - 1, TILES, 8, 128), F32),
            pltpu.VMEM((PER_Z * NZ, 8, 128), F32),
            pltpu.VMEM((NZ - 1, PER_Z, 8, 128), F32),
            pltpu.VMEM((NY, NX, NC, PER_Z * NZ, 8, 128), F32),
            pltpu.VMEM(square, F32),
            pltpu.VMEM(square, BF16),
            pltpu.VMEM(square, BF16),
            pltpu.VMEM(square, F32),
            pltpu.VMEM(square, BF16),
            pltpu.VMEM(square, BF16),
            pltpu.VMEM(square, BF16),
            pltpu.VMEM(square, BF16),
            pltpu.VMEM((OWN_M * K, rows), BF16),
            pltpu.VMEM((K, rows), BF16),
            pltpu.VMEM((NX * NC, ROWS_K, K), F32),
            pltpu.VMEM((NX * NC - 1, ROWS_K, K), F32),
            pltpu.VMEM((NZ, 8, K), F32),
            pltpu.VMEM((NZ - 1, 8, K), F32),
            pltpu.SemaphoreType.DMA((copies,)),
            pltpu.SemaphoreType.DMA((copies,)),
            pltpu.SemaphoreType.DMA((4,)),
        ],
        compiler_params=pltpu.CompilerParams(
            collective_id=0, has_side_effects=True, vmem_limit_bytes=56 * 2**20
        ),
        name="rotate_and_refit",
    )(vectors, codes, codebook.T)
    return rotation, refit


def solution(mesh):
    placed = (P("dim", "dp"), P("dim", "dp"), P(None, "dim"))
    return jax.shard_map(
        per_device,
        mesh=mesh,
        in_specs=placed,
        out_specs=(P("dim", None), P("dp", "dim")),
        check_vma=False,
    )
```

```python
import jax
import jax.numpy as jnp
from jax import lax
from jax.experimental import pallas as pl
from jax.experimental.pallas import tpu as pltpu
from jax.sharding import PartitionSpec as P

NX, NZ, NC, NY = 4, 8, 2, 4
D, M, K = 768, 64, 256
SUB = D // M
OWN = D // NY
OWN_M = M // NY
TILES = 18
PER_Z = 3
HALF = TILES // 2
ROWS_K = K // NX // NC
MESH = pl.DeviceIdType.MESH
F32, BF16 = jnp.float32, jnp.bfloat16
NT = (((1,), (1,)), ((), ()))
NN = (((1,), (0,)), ((), ()))


def dot(a, b, dims):
    return lax.dot_general(a, b, dims, preferred_element_type=F32)


def split(value):
    high = value.astype(BF16)
    return high, (value - high.astype(F32)).astype(BF16)


def product(a_high, a_low, b_high, b_low, dims):
    return dot(a_high, b_high, dims) + (dot(a_high, b_low, dims) + dot(a_low, b_high, dims))


def position():
    dp = lax.axis_index("dp")
    y = lax.axis_index("dim")
    core = lax.rem(dp, NC)
    z = lax.rem(dp // NC, NZ)
    x = dp // (NC * NZ)
    return x, z, core, y


def device(x, z, core, y):
    return ((x * NZ + z) * NC + core, y)


def own_rows(y):
    return pl.ds(pl.multiple_of(y * OWN, 64), OWN)


def decode(codes_all, book_all, decoded, y, half):
    group = OWN_M // 2
    height = group * SUB
    rows = decoded.shape[1]
    which = lax.broadcasted_iota(jnp.int32, (height, 128), 0) // SUB
    book = book_all[y, half].astype(F32)
    low, high = book[:, :128], book[:, 128:]
    base = pl.multiple_of(y * OWN + half * height, 32)
    for block in range(rows // 128):
        cols = pl.ds(block * 128, 128)
        both = codes_all[y, :, cols].astype(F32).astype(jnp.int32)
        lines = jnp.where(half == 0, both[:group], both[group:])
        index = jnp.broadcast_to(lines[0:1], (height, 128))
        for s in range(1, group):
            line = jnp.broadcast_to(lines[s : s + 1], (height, 128))
            index = jnp.where(which == s, line, index)
        lane = index & 127
        picked = jnp.where(
            index >= 128,
            jnp.take_along_axis(high, lane, axis=1),
            jnp.take_along_axis(low, lane, axis=1),
        )
        decoded[pl.ds(base, height), cols] = picked.astype(BF16)


def newton(y, whole, a_high, a_low, h, h_high, h_low, t_high, t_low):
    squares = [jnp.zeros((8, 128), F32)] * 12
    for s in range(D // 8):
        for j in range(D // 128):
            tile = whole[s * 8 : s * 8 + 8, j * 128 : j * 128 + 128]
            n = s % 2 * 6 + j
            squares[n] = squares[n] + tile * tile
    energy = jnp.sum(sum(squares[1:], squares[0]))
    scale = 1.0 / energy
    side = 256
    count = D // side

    def cut(i):
        return slice(i * side, i * side + side)

    for i in range(count):
        a_high[cut(i)], a_low[cut(i)] = split(whole[cut(i)])

    start = pl.multiple_of(y * OWN - 64 * lax.rem(y, 2), 128)
    own = whole[:, pl.ds(start, 256)]
    own = jnp.where(lax.rem(y, 2) == 1, pltpu.roll(own, 192, 1), own)
    own = own.T[:OWN] / jnp.sqrt(energy)

    upper = [(i, j) for i in range(count) for j in range(i, count)]

    def put(full, high, low, i, j, value):
        full[cut(i), cut(j)] = value
        high[cut(i), cut(j)], low[cut(i), cut(j)] = split(value)
        if i != j:
            high[cut(j), cut(i)], low[cut(j), cut(i)] = split(value.T)

    def times_h(value):
        high, low = split(value)
        return product(high, low, h_high[...], h_low[...], NN)

    for i, j in upper:
        value = product(a_high[cut(i)], a_low[cut(i)], a_high[cut(j)], a_low[cut(j)], NT)
        put(h, h_high, h_low, i, j, value * scale)
    for step in range(2):
        own = 1.5 * own - 0.5 * times_h(own)
        for i, j in upper:
            value = product(h_high[cut(i)], h_low[cut(i)], h_high[:, cut(j)], h_low[:, cut(j)], NN)
            put(whole, t_high, t_low, i, j, 1.5 * h[cut(i), cut(j)] - 0.5 * value)
        for i, j in upper:
            value = product(t_high[cut(i)], t_low[cut(i)], h_high[:, cut(j)], h_low[:, cut(j)], NN)
            h[cut(i), cut(j)] = 1.5 * whole[cut(i), cut(j)] - 0.5 * value
        for i, j in upper:
            put(h, h_high, h_low, i, j, h[cut(i), cut(j)])
    own = 1.5 * own - 0.5 * times_h(own)
    last = times_h(own)
    for _ in range(2):
        last = 1.5 * last - 0.5 * times_h(last)
    return 1.5 * own - 0.5 * last


def kernel(
    vectors_hbm, codes_hbm, book_hbm, rotation_hbm, refit_ref,
    codes_ref, rotation_ref, codes_all, book_all, vectors_all, decoded, part, box_core, sum_core, box_x, sum_x, box_z,
    full, whole, a_high, a_low, h, h_high, h_low, t_high, t_low,
    onehot, weights, sums, box_one, stage_two, box_two, send_sem, recv_sem, local_sem,
):
    x, z, core, y = position()
    rows = vectors_all.shape[1]
    sibling = device(x, z, 1 - core, y)
    across_x = [device(lax.rem(x + off, NX), z, core, y) for off in range(1, NX)]
    across_z = [device(x, lax.rem(z + off, NZ), core, y) for off in range(1, NZ)]
    across_y = [device(x, z, core, lax.rem(y + off, NY)) for off in range(1, NY)]
    other_x = [
        device(lax.rem(x + off, NX), z, 1 - core, y) for off in range(1, NX)
    ]
    sent = []
    number = [0]

    def send(src, dst, peer):
        k = number[0]
        number[0] += 1
        copy = pltpu.make_async_remote_copy(
            src_ref=src, dst_ref=dst, send_sem=send_sem.at[k], recv_sem=recv_sem.at[k],
            device_id=peer, device_id_type=MESH,
        )
        copy.start()
        sent.append(copy)
        return copy

    def spread(ref, peers):
        return [send(ref, ref, peer) for peer in peers]

    barrier = pltpu.get_barrier_semaphore()
    peers = [sibling] + across_x + other_x + across_z + across_y
    for peer in peers:
        pl.semaphore_signal(barrier, inc=1, device_id=peer, device_id_type=MESH)
    mine = vectors_all.at[own_rows(y), :]
    load_codes = pltpu.make_async_copy(codes_hbm, codes_ref, local_sem.at[0])
    load_book = pltpu.make_async_copy(book_hbm, book_all.at[y], local_sem.at[1])
    load_vectors = pltpu.make_async_copy(vectors_hbm, mine, local_sem.at[2])
    for copy in (load_codes, load_book, load_vectors):
        copy.start()
    stage_two[...] = jnp.zeros((NZ, 8, K), F32)
    weights[OWN:, :] = jnp.where(
        lax.broadcasted_iota(jnp.int32, (K - OWN, rows), 0) < OWN_M, 1.0, 0.0
    ).astype(BF16)
    load_codes.wait()
    codes_all[y] = codes_ref[...].astype(F32).astype(BF16)
    load_book.wait()
    load_vectors.wait()
    pl.semaphore_wait(barrier, len(peers))

    arrivals = []
    for peer in across_y:
        arrivals += spread(codes_all.at[y], [peer]) + spread(book_all.at[y, core], [peer])
    decode(codes_all, book_all, decoded, y, core)
    decode(codes_all, book_all, decoded, y, 1 - core)
    sources = [lax.rem(y + NY - 1 - i, NY) for i in range(NY - 1)]
    passed = []
    for i, source in enumerate(sources):
        arrivals[2 * i].wait_recv()
        arrivals[2 * i + 1].wait_recv()
        passed += spread(book_all.at[source, core], [sibling])
        decode(codes_all, book_all, decoded, source, core)
    for i, source in enumerate(sources):
        passed[i].wait_recv()
        decode(codes_all, book_all, decoded, source, 1 - core)
    vectors_here = spread(mine, across_y)

    value = dot(vectors_all[own_rows(y), :], decoded[...], NT)
    for pair in range(NX * NC):
        for t in range(TILES):
            i, j = pair * 3 + t // 6, t % 6
            part[pair // NC, pair % NC, t] = value[i * 8 : i * 8 + 8, j * 128 : j * 128 + 128]

    order = [lax.rem(x + off, NX) for off in (1, 2, 3, 0)]
    first = [send(part.at[i, 1 - core], box_core.at[i], sibling) for i in order]
    stage = []
    for n, copy in enumerate(first):
        i = order[n]
        copy.wait_recv()
        sum_core[i] = part[i, core] + box_core[i]
        if n < NX - 1:
            stage.append(send(sum_core.at[i], box_x.at[n], across_x[n]))
    place = lax.broadcasted_iota(jnp.int32, (ROWS_K, rows), 0)
    level = place // 4 * 8 + place % 4
    for m in range(OWN_M):
        code = jnp.broadcast_to(codes_ref[m : m + 1, :], (ROWS_K, rows))
        for chunk in range(NX * NC):
            at = (chunk * OWN_M + m) * ROWS_K
            same = level == code - (chunk // NC * 64 + chunk % NC * 4)
            onehot[at : at + ROWS_K] = jnp.where(same, 1.0, 0.0).astype(BF16)
    for copy in stage:
        copy.wait_recv()
    sum_x[:TILES] = (sum_core[x] + box_x[0]) + (box_x[1] + box_x[2])
    shared = TILES // PER_Z
    first_z = number[0]
    number[0] += 2 * (NZ - 1)

    def along_z(k, src, dst, i):
        return pltpu.make_async_remote_copy(
            src_ref=src, dst_ref=dst,
            send_sem=send_sem.at[first_z + k], recv_sem=recv_sem.at[first_z + k],
            device_id=across_z[i], device_id_type=MESH,
        )

    def part_copy(i):
        share = pl.ds(lax.rem(z + i + 1, NZ) * PER_Z, PER_Z)
        return along_z(i, sum_x.at[share], box_z.at[i], i)

    share = pl.ds(z * PER_Z, PER_Z)

    def total_copy(i):
        own = full.at[y, x, core, share]
        return along_z(NZ - 1 + i, own, own, i)

    for i in range(NZ - 1):
        @pl.when(lax.rem(z + i + 1, NZ) < shared)
        def _():
            part_copy(i).start()

    @pl.when(z < shared)
    def _():
        for i in range(NZ - 1):
            part_copy(i).wait_recv()
        total = sum_x[share]
        for i in range(NZ - 1):
            total = total + box_z[i]
        full[y, x, core, share] = total
        for i in range(NZ - 1):
            total_copy(i).start()

    for i in range(NZ - 1):
        @pl.when(lax.rem(z + NZ - i - 1, NZ) < shared)
        def _():
            total_copy(i).wait_recv()

    def piece(y, x, core, half):
        return full.at[y, x, core, pl.ds(half * HALF, HALF)]

    def lay(y, x, core, half):
        base = ((y * NX + x) * NC + core) * 24
        for t in range(half * HALF, half * HALF + HALF):
            row = pl.multiple_of(base + t // 6 * 8, 8)
            col = t % 6 * 128
            whole[pl.ds(row, 8), col : col + 128] = full[y, x, core, t]

    def before(index, off, size):
        return lax.rem(index + size - off, size)

    one, two = piece(y, x, core, 0), piece(y, x, core, 1)
    one_x, two_y = spread(one, across_x), spread(two, across_y)
    one_y, two_x = [spread(one, across_y)], [spread(two, across_x)]
    siblings = [(spread(one, [sibling])[0], y, x, 0), (spread(two, [sibling])[0], y, x, 1)]
    lay(y, x, core, 0)
    lay(y, x, core, 1)
    for i in range(NX - 1):
        from_x = before(x, i + 1, NX)
        one_x[i].wait_recv()
        ref = piece(y, from_x, core, 0)
        one_y.append(spread(ref, across_y))
        siblings.append((spread(ref, [sibling])[0], y, from_x, 0))
        from_y = before(y, i + 1, NY)
        two_y[i].wait_recv()
        ref = piece(from_y, x, core, 1)
        two_x.append(spread(ref, across_x))
        siblings.append((spread(ref, [sibling])[0], from_y, x, 1))
        lay(y, from_x, core, 0)
        lay(from_y, x, core, 1)
    for n in range(NX):
        for i in range(NX - 1):
            at_x, at_y = before(x, n, NX), before(y, i + 1, NY)
            one_y[n][i].wait_recv()
            siblings.append((spread(piece(at_y, at_x, core, 0), [sibling])[0], at_y, at_x, 0))
            lay(at_y, at_x, core, 0)
            at_x, at_y = before(x, i + 1, NX), before(y, n, NY)
            two_x[n][i].wait_recv()
            siblings.append((spread(piece(at_y, at_x, core, 1), [sibling])[0], at_y, at_x, 1))
            lay(at_y, at_x, core, 1)
    for copy, at_y, at_x, half in siblings:
        copy.wait_recv()
        lay(at_y, at_x, 1 - core, half)

    rotation = newton(y, whole, a_high, a_low, h, h_high, h_low, t_high, t_low)
    rotation_ref[...] = rotation
    store_rotation = pltpu.make_async_copy(rotation_ref, rotation_hbm, local_sem.at[3])
    store_rotation.start()

    for copy in vectors_here:
        copy.wait_recv()
    rotated = dot(rotation.astype(BF16), vectors_all[...], NN)
    weights[:OWN, :] = rotated.astype(BF16)
    column = lax.broadcasted_iota(jnp.int32, (ROWS_K, K), 1)
    subspace = jnp.where(column < OWN, column // SUB, column - OWN)

    stage = []
    height = OWN_M * ROWS_K
    for n, (off, flip) in enumerate(((2, 0), (2, 1), (1, 0), (1, 1), (3, 0), (3, 1), (0, 1), (0, 0))):
        to_x, to_core = lax.rem(x + off, NX), lax.rem(core + flip, NC)
        chunk = pl.multiple_of((to_x * NC + to_core) * height, height)
        value = dot(onehot[pl.ds(chunk, height)], weights[...], NT)
        total = jnp.zeros((ROWS_K, K), F32)
        for m in range(OWN_M):
            total = jnp.where(subspace == m, value[m * ROWS_K : (m + 1) * ROWS_K], total)
        sums[n] = total
        if n < NX * NC - 1:
            stage.append(send(sums.at[n], box_one.at[n], device(to_x, z, to_core, y)))
    for copy in stage:
        copy.wait_recv()
    total = sums[NX * NC - 1]
    for i in range(len(stage)):
        total = total + box_one[i]
    for i in range(NZ):
        stage_two[i, 0:4] = total[i * 4 : i * 4 + 4]
    stage = [
        send(stage_two.at[lax.rem(z + i + 1, NZ)], box_two.at[i], peer)
        for i, peer in enumerate(across_z)
    ]
    for copy in stage:
        copy.wait_recv()
    total = stage_two[z]
    for i in range(NZ - 1):
        total = total + box_two[i]
    refit_ref[...] = total
    for copy in sent:
        copy.wait_send()
    for i in range(NZ - 1):
        @pl.when(lax.rem(z + i + 1, NZ) < shared)
        def _():
            part_copy(i).wait_send()
        @pl.when(z < shared)
        def _():
            total_copy(i).wait_send()
    store_rotation.wait()


def finish_kernel(rotation_ref, totals_ref, out_ref, refit_ref):
    out_ref[...] = rotation_ref[...]
    total = totals_ref[...]
    left, right = total[:, :128], total[:, 128:]
    lane = lax.broadcasted_iota(jnp.int32, (8, 128), 1)
    offset = OWN - 128
    count = jnp.take_along_axis(right, offset + lane // SUB, axis=1)
    refit_ref[:, :128] = (left / jnp.maximum(count, 1.0))[0:4]
    count = jnp.take_along_axis(right, offset + jnp.minimum((lane + 128) // SUB, OWN_M - 1), axis=1)
    refit_ref[:, 128:] = (right / jnp.maximum(count, 1.0))[0:4, :offset]


def per_device(vectors, codes, codebook):
    rows = vectors.shape[1]
    vmem = pl.BlockSpec(memory_space=pltpu.VMEM)
    anywhere = pl.BlockSpec(memory_space=pl.ANY)
    square = (D, D)
    copies = 9 + 3 + 4 + 3 + 7 + 7 + 12 + 2 + 24 + 24 + 7 + 7
    rotation, totals = pl.pallas_call(
        kernel,
        out_shape=(
            jax.ShapeDtypeStruct((OWN, D), F32),
            jax.ShapeDtypeStruct((8, K), F32),
        ),
        in_specs=[anywhere] * 3,
        out_specs=(anywhere, vmem),
        scratch_shapes=[
            pltpu.VMEM((OWN_M, rows), jnp.int32),
            pltpu.VMEM((OWN, D), F32),
            pltpu.VMEM((NY, OWN_M, rows), BF16),
            pltpu.VMEM((NY, 2, OWN // 2, K), BF16),
            pltpu.VMEM((D, rows), BF16),
            pltpu.VMEM((D, rows), BF16),
            pltpu.VMEM((NX, NC, TILES, 8, 128), F32),
            pltpu.VMEM((NX, TILES, 8, 128), F32),
            pltpu.VMEM((NX, TILES, 8, 128), F32),
            pltpu.VMEM((NX - 1, TILES, 8, 128), F32),
            pltpu.VMEM((PER_Z * NZ, 8, 128), F32),
            pltpu.VMEM((NZ - 1, PER_Z, 8, 128), F32),
            pltpu.VMEM((NY, NX, NC, PER_Z * NZ, 8, 128), F32),
            pltpu.VMEM(square, F32),
            pltpu.VMEM(square, BF16),
            pltpu.VMEM(square, BF16),
            pltpu.VMEM(square, F32),
            pltpu.VMEM(square, BF16),
            pltpu.VMEM(square, BF16),
            pltpu.VMEM(square, BF16),
            pltpu.VMEM(square, BF16),
            pltpu.VMEM((OWN_M * K, rows), BF16),
            pltpu.VMEM((K, rows), BF16),
            pltpu.VMEM((NX * NC, ROWS_K, K), F32),
            pltpu.VMEM((NX * NC - 1, ROWS_K, K), F32),
            pltpu.VMEM((NZ, 8, K), F32),
            pltpu.VMEM((NZ - 1, 8, K), F32),
            pltpu.SemaphoreType.DMA((copies,)),
            pltpu.SemaphoreType.DMA((copies,)),
            pltpu.SemaphoreType.DMA((4,)),
        ],
        compiler_params=pltpu.CompilerParams(
            collective_id=0, has_side_effects=True, vmem_limit_bytes=56 * 2**20
        ),
        name="rotate_and_refit",
    )(vectors, codes, codebook.T.reshape(2, OWN // 2, K))
    return pl.pallas_call(
        finish_kernel,
        out_shape=(
            jax.ShapeDtypeStruct((OWN, D), F32),
            jax.ShapeDtypeStruct((K // (NX * NZ * NC), OWN), F32),
        ),
        in_specs=[vmem, vmem],
        out_specs=(vmem, vmem),
        name="finish",
    )(rotation, totals)


def solution(mesh):
    placed = (P("dim", "dp"), P("dim", "dp"), P(None, "dim"))
    return jax.shard_map(
        per_device,
        mesh=mesh,
        in_specs=placed,
        out_specs=(P("dim", None), P("dp", "dim")),
        check_vma=False,
    )
```

```python
import jax
import jax.numpy as jnp
from jax import lax
from jax.experimental import pallas as pl
from jax.experimental.pallas import tpu as pltpu
from jax.sharding import PartitionSpec as P

NX, NZ, NC, NY = 4, 8, 2, 4
D, M, K = 768, 64, 256
SUB = D // M
OWN = D // NY
OWN_M = M // NY
TILES = 18
PER_Z = 3
HALF = TILES // 2
ROWS_K = K // NX // NC
FOUR = (2, 1, 3)
EIGHT = (4, 3, 5, 2, 6, 1, 7)
MESH = pl.DeviceIdType.MESH
F32, BF16 = jnp.float32, jnp.bfloat16
NT = (((1,), (1,)), ((), ()))
NN = (((1,), (0,)), ((), ()))


def dot(a, b, dims):
    return lax.dot_general(a, b, dims, preferred_element_type=F32)


def split(value):
    high = value.astype(BF16)
    return high, (value - high.astype(F32)).astype(BF16)


def product(a_high, a_low, b_high, b_low, dims):
    return dot(a_high, b_high, dims) + (dot(a_high, b_low, dims) + dot(a_low, b_high, dims))


def position():
    dp = lax.axis_index("dp")
    y = lax.axis_index("dim")
    core = lax.rem(dp, NC)
    z = lax.rem(dp // NC, NZ)
    x = dp // (NC * NZ)
    return x, z, core, y


def device(x, z, core, y):
    return ((x * NZ + z) * NC + core, y)


def own_rows(y):
    return pl.ds(pl.multiple_of(y * OWN, 64), OWN)


def decode(codes_all, book_all, decoded, y, half):
    group = OWN_M // 2
    height = group * SUB
    rows = decoded.shape[1]
    which = lax.broadcasted_iota(jnp.int32, (height, 128), 0) // SUB
    book = book_all[y, half].astype(F32)
    low, high = book[:, :128], book[:, 128:]
    base = pl.multiple_of(y * OWN + half * height, 32)
    for block in range(rows // 128):
        cols = pl.ds(block * 128, 128)
        both = codes_all[y, :, cols].astype(F32).astype(jnp.int32)
        lines = jnp.where(half == 0, both[:group], both[group:])
        index = jnp.broadcast_to(lines[0:1], (height, 128))
        for s in range(1, group):
            line = jnp.broadcast_to(lines[s : s + 1], (height, 128))
            index = jnp.where(which == s, line, index)
        lane = index & 127
        picked = jnp.where(
            index >= 128,
            jnp.take_along_axis(high, lane, axis=1),
            jnp.take_along_axis(low, lane, axis=1),
        )
        decoded[pl.ds(base, height), cols] = picked.astype(BF16)


def newton(y, whole, a_high, a_low, h, h_high, h_low, t_high, t_low):
    squares = [jnp.zeros((8, 128), F32)] * 12
    for s in range(D // 8):
        for j in range(D // 128):
            tile = whole[s * 8 : s * 8 + 8, j * 128 : j * 128 + 128]
            n = s % 2 * 6 + j
            squares[n] = squares[n] + tile * tile
    energy = jnp.sum(sum(squares[1:], squares[0]))
    scale = 1.0 / energy
    side = 256
    count = D // side

    def cut(i):
        return slice(i * side, i * side + side)

    for i in range(count):
        a_high[cut(i)], a_low[cut(i)] = split(whole[cut(i)])

    start = pl.multiple_of(y * OWN - 64 * lax.rem(y, 2), 128)
    own = whole[:, pl.ds(start, 256)]
    own = jnp.where(lax.rem(y, 2) == 1, pltpu.roll(own, 192, 1), own)
    own = own.T[:OWN] / jnp.sqrt(energy)

    upper = [(i, j) for i in range(count) for j in range(i, count)]

    def put(full, high, low, i, j, value):
        full[cut(i), cut(j)] = value
        high[cut(i), cut(j)], low[cut(i), cut(j)] = split(value)
        if i != j:
            high[cut(j), cut(i)], low[cut(j), cut(i)] = split(value.T)

    def times_h(value):
        high, low = split(value)
        return product(high, low, h_high[...], h_low[...], NN)

    for i, j in upper:
        value = product(a_high[cut(i)], a_low[cut(i)], a_high[cut(j)], a_low[cut(j)], NT)
        put(h, h_high, h_low, i, j, value * scale)
    for step in range(2):
        own = 1.5 * own - 0.5 * times_h(own)
        for i, j in upper:
            value = product(h_high[cut(i)], h_low[cut(i)], h_high[:, cut(j)], h_low[:, cut(j)], NN)
            put(whole, t_high, t_low, i, j, 1.5 * h[cut(i), cut(j)] - 0.5 * value)
        for i, j in upper:
            value = product(t_high[cut(i)], t_low[cut(i)], h_high[:, cut(j)], h_low[:, cut(j)], NN)
            h[cut(i), cut(j)] = 1.5 * whole[cut(i), cut(j)] - 0.5 * value
        for i, j in upper:
            put(h, h_high, h_low, i, j, h[cut(i), cut(j)])
    own = 1.5 * own - 0.5 * times_h(own)
    last = times_h(own)
    for _ in range(2):
        last = 1.5 * last - 0.5 * times_h(last)
    return 1.5 * own - 0.5 * last


def kernel(
    vectors_hbm, codes_hbm, book_hbm, rotation_hbm, refit_ref,
    codes_ref, rotation_ref, codes_all, book_all, vectors_all, decoded, part, box_core, sum_core, box_x, sum_x, box_z,
    full, whole, a_high, a_low, h, h_high, h_low, t_high, t_low,
    onehot, weights, sums, box_one, stage_two, box_two, send_sem, recv_sem, local_sem,
):
    x, z, core, y = position()
    rows = vectors_all.shape[1]
    sibling = device(x, z, 1 - core, y)
    across_x = [device(lax.rem(x + off, NX), z, core, y) for off in FOUR]
    across_z = [device(x, lax.rem(z + off, NZ), core, y) for off in EIGHT]
    across_y = [device(x, z, core, lax.rem(y + off, NY)) for off in FOUR]
    other_x = [
        device(lax.rem(x + off, NX), z, 1 - core, y) for off in range(1, NX)
    ]
    sent = []
    number = [0]

    def send(src, dst, peer):
        k = number[0]
        number[0] += 1
        copy = pltpu.make_async_remote_copy(
            src_ref=src, dst_ref=dst, send_sem=send_sem.at[k], recv_sem=recv_sem.at[k],
            device_id=peer, device_id_type=MESH,
        )
        copy.start()
        sent.append(copy)
        return copy

    def spread(ref, peers):
        return [send(ref, ref, peer) for peer in peers]

    barrier = pltpu.get_barrier_semaphore()
    peers = [sibling] + across_x + other_x + across_z + across_y
    for peer in peers:
        pl.semaphore_signal(barrier, inc=1, device_id=peer, device_id_type=MESH)
    mine = vectors_all.at[own_rows(y), :]
    load_codes = pltpu.make_async_copy(codes_hbm, codes_ref, local_sem.at[0])
    load_book = pltpu.make_async_copy(book_hbm, book_all.at[y], local_sem.at[1])
    load_vectors = pltpu.make_async_copy(vectors_hbm, mine, local_sem.at[2])
    for copy in (load_codes, load_book, load_vectors):
        copy.start()
    stage_two[...] = jnp.zeros((NZ, 8, K), F32)
    weights[OWN:, :] = jnp.where(
        lax.broadcasted_iota(jnp.int32, (K - OWN, rows), 0) < OWN_M, 1.0, 0.0
    ).astype(BF16)
    load_codes.wait()
    codes_all[y] = codes_ref[...].astype(F32).astype(BF16)
    load_book.wait()
    load_vectors.wait()
    pl.semaphore_wait(barrier, len(peers))

    arrivals = []
    for peer in across_y:
        arrivals += spread(codes_all.at[y], [peer]) + spread(book_all.at[y, core], [peer])
    decode(codes_all, book_all, decoded, y, core)
    decode(codes_all, book_all, decoded, y, 1 - core)
    sources = [lax.rem(y + NY - off, NY) for off in FOUR]
    passed = []
    for i, source in enumerate(sources):
        arrivals[2 * i].wait_recv()
        arrivals[2 * i + 1].wait_recv()
        passed += spread(book_all.at[source, core], [sibling])
        decode(codes_all, book_all, decoded, source, core)
    for i, source in enumerate(sources):
        passed[i].wait_recv()
        decode(codes_all, book_all, decoded, source, 1 - core)
    vectors_here = spread(mine, across_y)

    value = dot(vectors_all[own_rows(y), :], decoded[...], NT)
    for pair in range(NX * NC):
        for t in range(TILES):
            i, j = pair * 3 + t // 6, t % 6
            part[pair // NC, pair % NC, t] = value[i * 8 : i * 8 + 8, j * 128 : j * 128 + 128]

    order = [lax.rem(x + off, NX) for off in FOUR + (0,)]
    first = [send(part.at[i, 1 - core], box_core.at[i], sibling) for i in order]
    stage = []
    for n, copy in enumerate(first):
        i = order[n]
        copy.wait_recv()
        sum_core[i] = part[i, core] + box_core[i]
        if n < NX - 1:
            stage.append(send(sum_core.at[i], box_x.at[n], across_x[n]))
    place = lax.broadcasted_iota(jnp.int32, (ROWS_K, rows), 0)
    level = place // 4 * 8 + place % 4
    for m in range(OWN_M):
        code = jnp.broadcast_to(codes_ref[m : m + 1, :], (ROWS_K, rows))
        for chunk in range(NX * NC):
            at = (chunk * OWN_M + m) * ROWS_K
            same = level == code - (chunk // NC * 64 + chunk % NC * 4)
            onehot[at : at + ROWS_K] = jnp.where(same, 1.0, 0.0).astype(BF16)
    for copy in stage:
        copy.wait_recv()
    sum_x[:TILES] = (sum_core[x] + box_x[0]) + (box_x[1] + box_x[2])
    shared = TILES // PER_Z
    first_z = number[0]
    number[0] += 2 * (NZ - 1)

    def along_z(k, src, dst, i):
        return pltpu.make_async_remote_copy(
            src_ref=src, dst_ref=dst,
            send_sem=send_sem.at[first_z + k], recv_sem=recv_sem.at[first_z + k],
            device_id=across_z[i], device_id_type=MESH,
        )

    def part_copy(i):
        share = pl.ds(lax.rem(z + EIGHT[i], NZ) * PER_Z, PER_Z)
        return along_z(i, sum_x.at[share], box_z.at[i], i)

    share = pl.ds(z * PER_Z, PER_Z)

    def total_copy(i):
        own = full.at[y, x, core, share]
        return along_z(NZ - 1 + i, own, own, i)

    for i in range(NZ - 1):
        @pl.when(lax.rem(z + EIGHT[i], NZ) < shared)
        def _():
            part_copy(i).start()

    @pl.when(z < shared)
    def _():
        for i in range(NZ - 1):
            part_copy(i).wait_recv()
        total = sum_x[share]
        for i in range(NZ - 1):
            total = total + box_z[i]
        full[y, x, core, share] = total
        for i in range(NZ - 1):
            total_copy(i).start()

    for i in range(NZ - 1):
        @pl.when(lax.rem(z + NZ - EIGHT[i], NZ) < shared)
        def _():
            total_copy(i).wait_recv()

    def piece(y, x, core, half):
        return full.at[y, x, core, pl.ds(half * HALF, HALF)]

    def lay(y, x, core, half):
        base = ((y * NX + x) * NC + core) * 24
        for t in range(half * HALF, half * HALF + HALF):
            row = pl.multiple_of(base + t // 6 * 8, 8)
            col = t % 6 * 128
            whole[pl.ds(row, 8), col : col + 128] = full[y, x, core, t]

    def before(index, off, size):
        return lax.rem(index + size - off, size)

    steps = (0,) + FOUR

    one, two = piece(y, x, core, 0), piece(y, x, core, 1)
    one_x, two_y = spread(one, across_x), spread(two, across_y)
    one_y, two_x = [spread(one, across_y)], [spread(two, across_x)]
    siblings = [(spread(one, [sibling])[0], y, x, 0), (spread(two, [sibling])[0], y, x, 1)]
    lay(y, x, core, 0)
    lay(y, x, core, 1)
    for i in range(NX - 1):
        from_x = before(x, FOUR[i], NX)
        one_x[i].wait_recv()
        ref = piece(y, from_x, core, 0)
        one_y.append(spread(ref, across_y))
        siblings.append((spread(ref, [sibling])[0], y, from_x, 0))
        from_y = before(y, FOUR[i], NY)
        two_y[i].wait_recv()
        ref = piece(from_y, x, core, 1)
        two_x.append(spread(ref, across_x))
        siblings.append((spread(ref, [sibling])[0], from_y, x, 1))
        lay(y, from_x, core, 0)
        lay(from_y, x, core, 1)
    for n in range(NX):
        for i in range(NX - 1):
            at_x, at_y = before(x, steps[n], NX), before(y, FOUR[i], NY)
            one_y[n][i].wait_recv()
            siblings.append((spread(piece(at_y, at_x, core, 0), [sibling])[0], at_y, at_x, 0))
            lay(at_y, at_x, core, 0)
            at_x, at_y = before(x, FOUR[i], NX), before(y, steps[n], NY)
            two_x[n][i].wait_recv()
            siblings.append((spread(piece(at_y, at_x, core, 1), [sibling])[0], at_y, at_x, 1))
            lay(at_y, at_x, core, 1)
    for copy, at_y, at_x, half in siblings:
        copy.wait_recv()
        lay(at_y, at_x, 1 - core, half)

    rotation = newton(y, whole, a_high, a_low, h, h_high, h_low, t_high, t_low)
    rotation_ref[...] = rotation
    store_rotation = pltpu.make_async_copy(rotation_ref, rotation_hbm, local_sem.at[3])
    store_rotation.start()

    for copy in vectors_here:
        copy.wait_recv()
    rotated = dot(rotation.astype(BF16), vectors_all[...], NN)
    weights[:OWN, :] = rotated.astype(BF16)
    column = lax.broadcasted_iota(jnp.int32, (ROWS_K, K), 1)
    subspace = jnp.where(column < OWN, column // SUB, column - OWN)

    stage = []
    height = OWN_M * ROWS_K
    for n, (off, flip) in enumerate(((2, 0), (2, 1), (1, 0), (1, 1), (3, 0), (3, 1), (0, 1), (0, 0))):
        to_x, to_core = lax.rem(x + off, NX), lax.rem(core + flip, NC)
        chunk = pl.multiple_of((to_x * NC + to_core) * height, height)
        value = dot(onehot[pl.ds(chunk, height)], weights[...], NT)
        total = jnp.zeros((ROWS_K, K), F32)
        for m in range(OWN_M):
            total = jnp.where(subspace == m, value[m * ROWS_K : (m + 1) * ROWS_K], total)
        sums[n] = total
        if n < NX * NC - 1:
            stage.append(send(sums.at[n], box_one.at[n], device(to_x, z, to_core, y)))
    for copy in stage:
        copy.wait_recv()
    total = sums[NX * NC - 1]
    for i in range(len(stage)):
        total = total + box_one[i]
    for i in range(NZ):
        stage_two[i, 0:4] = total[i * 4 : i * 4 + 4]
    stage = [
        send(stage_two.at[lax.rem(z + EIGHT[i], NZ)], box_two.at[i], peer)
        for i, peer in enumerate(across_z)
    ]
    for copy in stage:
        copy.wait_recv()
    total = stage_two[z]
    for i in range(NZ - 1):
        total = total + box_two[i]
    refit_ref[...] = total
    for copy in sent:
        copy.wait_send()
    for i in range(NZ - 1):
        @pl.when(lax.rem(z + EIGHT[i], NZ) < shared)
        def _():
            part_copy(i).wait_send()
        @pl.when(z < shared)
        def _():
            total_copy(i).wait_send()
    store_rotation.wait()


def finish_kernel(rotation_ref, totals_ref, out_ref, refit_ref):
    out_ref[...] = rotation_ref[...]
    total = totals_ref[...]
    left, right = total[:, :128], total[:, 128:]
    lane = lax.broadcasted_iota(jnp.int32, (8, 128), 1)
    offset = OWN - 128
    count = jnp.take_along_axis(right, offset + lane // SUB, axis=1)
    refit_ref[:, :128] = (left / jnp.maximum(count, 1.0))[0:4]
    count = jnp.take_along_axis(right, offset + jnp.minimum((lane + 128) // SUB, OWN_M - 1), axis=1)
    refit_ref[:, 128:] = (right / jnp.maximum(count, 1.0))[0:4, :offset]


def per_device(vectors, codes, codebook):
    rows = vectors.shape[1]
    vmem = pl.BlockSpec(memory_space=pltpu.VMEM)
    anywhere = pl.BlockSpec(memory_space=pl.ANY)
    square = (D, D)
    copies = 9 + 3 + 4 + 3 + 7 + 7 + 12 + 2 + 24 + 24 + 7 + 7
    rotation, totals = pl.pallas_call(
        kernel,
        out_shape=(
            jax.ShapeDtypeStruct((OWN, D), F32),
            jax.ShapeDtypeStruct((8, K), F32),
        ),
        in_specs=[anywhere] * 3,
        out_specs=(anywhere, vmem),
        scratch_shapes=[
            pltpu.VMEM((OWN_M, rows), jnp.int32),
            pltpu.VMEM((OWN, D), F32),
            pltpu.VMEM((NY, OWN_M, rows), BF16),
            pltpu.VMEM((NY, 2, OWN // 2, K), BF16),
            pltpu.VMEM((D, rows), BF16),
            pltpu.VMEM((D, rows), BF16),
            pltpu.VMEM((NX, NC, TILES, 8, 128), F32),
            pltpu.VMEM((NX, TILES, 8, 128), F32),
            pltpu.VMEM((NX, TILES, 8, 128), F32),
            pltpu.VMEM((NX - 1, TILES, 8, 128), F32),
            pltpu.VMEM((PER_Z * NZ, 8, 128), F32),
            pltpu.VMEM((NZ - 1, PER_Z, 8, 128), F32),
            pltpu.VMEM((NY, NX, NC, PER_Z * NZ, 8, 128), F32),
            pltpu.VMEM(square, F32),
            pltpu.VMEM(square, BF16),
            pltpu.VMEM(square, BF16),
            pltpu.VMEM(square, F32),
            pltpu.VMEM(square, BF16),
            pltpu.VMEM(square, BF16),
            pltpu.VMEM(square, BF16),
            pltpu.VMEM(square, BF16),
            pltpu.VMEM((OWN_M * K, rows), BF16),
            pltpu.VMEM((K, rows), BF16),
            pltpu.VMEM((NX * NC, ROWS_K, K), F32),
            pltpu.VMEM((NX * NC - 1, ROWS_K, K), F32),
            pltpu.VMEM((NZ, 8, K), F32),
            pltpu.VMEM((NZ - 1, 8, K), F32),
            pltpu.SemaphoreType.DMA((copies,)),
            pltpu.SemaphoreType.DMA((copies,)),
            pltpu.SemaphoreType.DMA((4,)),
        ],
        compiler_params=pltpu.CompilerParams(
            collective_id=0, has_side_effects=True, vmem_limit_bytes=56 * 2**20
        ),
        name="rotate_and_refit",
    )(vectors, codes, codebook.T.reshape(2, OWN // 2, K))
    return pl.pallas_call(
        finish_kernel,
        out_shape=(
            jax.ShapeDtypeStruct((OWN, D), F32),
            jax.ShapeDtypeStruct((K // (NX * NZ * NC), OWN), F32),
        ),
        in_specs=[vmem, vmem],
        out_specs=(vmem, vmem),
        name="finish",
    )(rotation, totals)


def solution(mesh):
    placed = (P("dim", "dp"), P("dim", "dp"), P(None, "dim"))
    return jax.shard_map(
        per_device,
        mesh=mesh,
        in_specs=placed,
        out_specs=(P("dim", None), P("dp", "dim")),
        check_vma=False,
    )
```

```python
import jax
import jax.numpy as jnp
from jax import lax
from jax.experimental import pallas as pl
from jax.experimental.pallas import tpu as pltpu
from jax.sharding import PartitionSpec as P

NX, NZ, NC, NY = 4, 8, 2, 4
D, M, K = 768, 64, 256
SUB = D // M
OWN = D // NY
OWN_M = M // NY
TILES = 18
PER_Z = 3
HALF = TILES // 2
ROWS_K = K // NX // NC
FOUR = (2, 1, 3)
EIGHT = (4, 3, 5, 2, 6, 1, 7)
MESH = pl.DeviceIdType.MESH
F32, BF16 = jnp.float32, jnp.bfloat16
NT = (((1,), (1,)), ((), ()))
NN = (((1,), (0,)), ((), ()))


def dot(a, b, dims):
    return lax.dot_general(a, b, dims, preferred_element_type=F32)


def split(value):
    high = value.astype(BF16)
    return high, (value - high.astype(F32)).astype(BF16)


def product(a_high, a_low, b_high, b_low, dims):
    return dot(a_high, b_high, dims) + (dot(a_high, b_low, dims) + dot(a_low, b_high, dims))


def position():
    dp = lax.axis_index("dp")
    y = lax.axis_index("dim")
    core = lax.rem(dp, NC)
    z = lax.rem(dp // NC, NZ)
    x = dp // (NC * NZ)
    return x, z, core, y


def device(x, z, core, y):
    return ((x * NZ + z) * NC + core, y)


def own_rows(y):
    return pl.ds(pl.multiple_of(y * OWN, 64), OWN)


def decode(codes_all, book_all, decoded, y, half):
    group = OWN_M // 2
    height = group * SUB
    rows = decoded.shape[1]
    which = lax.broadcasted_iota(jnp.int32, (height, 128), 0) // SUB
    book = book_all[y, half].astype(F32)
    low, high = book[:, :128], book[:, 128:]
    base = pl.multiple_of(y * OWN + half * height, 32)
    for block in range(rows // 128):
        cols = pl.ds(block * 128, 128)
        both = codes_all[y, :, cols].astype(F32).astype(jnp.int32)
        lines = jnp.where(half == 0, both[:group], both[group:])
        index = jnp.broadcast_to(lines[0:1], (height, 128))
        for s in range(1, group):
            line = jnp.broadcast_to(lines[s : s + 1], (height, 128))
            index = jnp.where(which == s, line, index)
        lane = index & 127
        picked = jnp.where(
            index >= 128,
            jnp.take_along_axis(high, lane, axis=1),
            jnp.take_along_axis(low, lane, axis=1),
        )
        decoded[pl.ds(base, height), cols] = picked.astype(BF16)


def newton(y, whole, a_high, a_low, h, h_high, h_low, t_high, t_low):
    squares = [jnp.zeros((8, 128), F32)] * 12
    for s in range(D // 8):
        for j in range(D // 128):
            tile = whole[s * 8 : s * 8 + 8, j * 128 : j * 128 + 128]
            n = s % 2 * 6 + j
            squares[n] = squares[n] + tile * tile
    energy = jnp.sum(sum(squares[1:], squares[0]))
    scale = 1.0 / energy
    side = 256
    count = D // side

    def cut(i):
        return slice(i * side, i * side + side)

    for i in range(count):
        a_high[cut(i)], a_low[cut(i)] = split(whole[cut(i)])

    start = pl.multiple_of(y * OWN - 64 * lax.rem(y, 2), 128)
    own = whole[:, pl.ds(start, 256)]
    own = jnp.where(lax.rem(y, 2) == 1, pltpu.roll(own, 192, 1), own)
    own = own.T[:OWN] / jnp.sqrt(energy)

    upper = [(i, j) for i in range(count) for j in range(i, count)]

    def put(full, high, low, i, j, value):
        full[cut(i), cut(j)] = value
        high[cut(i), cut(j)], low[cut(i), cut(j)] = split(value)
        if i != j:
            high[cut(j), cut(i)], low[cut(j), cut(i)] = split(value.T)

    def times_h(value):
        high, low = split(value)
        both = dot(jnp.concatenate([high, low], axis=0), h_high[...], NN)
        return both[:OWN] + (both[OWN:] + dot(high, h_low[...], NN))

    for i, j in upper:
        value = product(a_high[cut(i)], a_low[cut(i)], a_high[cut(j)], a_low[cut(j)], NT)
        put(h, h_high, h_low, i, j, value * scale)
    for step in range(2):
        own = 1.5 * own - 0.5 * times_h(own)
        for i, j in upper:
            value = product(h_high[cut(i)], h_low[cut(i)], h_high[:, cut(j)], h_low[:, cut(j)], NN)
            put(whole, t_high, t_low, i, j, 1.5 * h[cut(i), cut(j)] - 0.5 * value)
        for i, j in upper:
            value = product(t_high[cut(i)], t_low[cut(i)], h_high[:, cut(j)], h_low[:, cut(j)], NN)
            h[cut(i), cut(j)] = 1.5 * whole[cut(i), cut(j)] - 0.5 * value
        for i, j in upper:
            put(h, h_high, h_low, i, j, h[cut(i), cut(j)])
    own = 1.5 * own - 0.5 * times_h(own)
    last = times_h(own)
    for _ in range(2):
        last = 1.5 * last - 0.5 * times_h(last)
    return 1.5 * own - 0.5 * last


def kernel(
    vectors_hbm, codes_hbm, book_hbm, rotation_hbm, refit_ref,
    codes_ref, rotation_ref, codes_all, book_all, vectors_all, decoded, part, box_core, sum_core, box_x, sum_x, box_z,
    full, whole, a_high, a_low, h, h_high, h_low, t_high, t_low,
    onehot, weights, sums, box_one, stage_two, box_two, send_sem, recv_sem, local_sem,
):
    x, z, core, y = position()
    rows = vectors_all.shape[1]
    sibling = device(x, z, 1 - core, y)
    across_x = [device(lax.rem(x + off, NX), z, core, y) for off in FOUR]
    across_z = [device(x, lax.rem(z + off, NZ), core, y) for off in EIGHT]
    across_y = [device(x, z, core, lax.rem(y + off, NY)) for off in FOUR]
    other_x = [
        device(lax.rem(x + off, NX), z, 1 - core, y) for off in range(1, NX)
    ]
    sent = []
    number = [0]

    def send(src, dst, peer):
        k = number[0]
        number[0] += 1
        copy = pltpu.make_async_remote_copy(
            src_ref=src, dst_ref=dst, send_sem=send_sem.at[k], recv_sem=recv_sem.at[k],
            device_id=peer, device_id_type=MESH,
        )
        copy.start()
        sent.append(copy)
        return copy

    def spread(ref, peers):
        return [send(ref, ref, peer) for peer in peers]

    barrier = pltpu.get_barrier_semaphore()
    peers = across_z + other_x + across_x + across_y + [sibling]
    for peer in peers:
        pl.semaphore_signal(barrier, inc=1, device_id=peer, device_id_type=MESH)
    mine = vectors_all.at[own_rows(y), :]
    load_codes = pltpu.make_async_copy(codes_hbm, codes_ref, local_sem.at[0])
    load_book = pltpu.make_async_copy(book_hbm, book_all.at[y], local_sem.at[1])
    load_vectors = pltpu.make_async_copy(vectors_hbm, mine, local_sem.at[2])
    for copy in (load_codes, load_book, load_vectors):
        copy.start()
    stage_two[...] = jnp.zeros((NZ, 8, K), F32)
    weights[OWN:, :] = jnp.where(
        lax.broadcasted_iota(jnp.int32, (K - OWN, rows), 0) < OWN_M, 1.0, 0.0
    ).astype(BF16)
    load_codes.wait()
    codes_all[y] = codes_ref[...].astype(F32).astype(BF16)
    load_book.wait()
    load_vectors.wait()
    pl.semaphore_wait(barrier, len(peers))

    arrivals = []
    for peer in across_y:
        arrivals += spread(codes_all.at[y], [peer]) + spread(book_all.at[y, core], [peer])
    decode(codes_all, book_all, decoded, y, core)
    decode(codes_all, book_all, decoded, y, 1 - core)
    sources = [lax.rem(y + NY - off, NY) for off in FOUR]
    passed = []
    for i, source in enumerate(sources):
        arrivals[2 * i].wait_recv()
        arrivals[2 * i + 1].wait_recv()
        passed += spread(book_all.at[source, core], [sibling])
        decode(codes_all, book_all, decoded, source, core)
    for i, source in enumerate(sources):
        passed[i].wait_recv()
        decode(codes_all, book_all, decoded, source, 1 - core)
    vectors_here = spread(mine, across_y)

    value = dot(vectors_all[own_rows(y), :], decoded[...], NT)
    for pair in range(NX * NC):
        for t in range(TILES):
            i, j = pair * 3 + t // 6, t % 6
            part[pair // NC, pair % NC, t] = value[i * 8 : i * 8 + 8, j * 128 : j * 128 + 128]

    order = [lax.rem(x + off, NX) for off in FOUR + (0,)]
    first = [send(part.at[i, 1 - core], box_core.at[i], sibling) for i in order]
    stage = []
    for n, copy in enumerate(first):
        i = order[n]
        copy.wait_recv()
        sum_core[i] = part[i, core] + box_core[i]
        if n < NX - 1:
            stage.append(send(sum_core.at[i], box_x.at[n], across_x[n]))
    place = lax.broadcasted_iota(jnp.int32, (ROWS_K, rows), 0)
    level = place // 4 * 8 + place % 4
    for m in range(OWN_M):
        code = jnp.broadcast_to(codes_ref[m : m + 1, :], (ROWS_K, rows))
        for chunk in range(NX * NC):
            at = (chunk * OWN_M + m) * ROWS_K
            same = level == code - (chunk // NC * 64 + chunk % NC * 4)
            onehot[at : at + ROWS_K] = jnp.where(same, 1.0, 0.0).astype(BF16)
    for copy in stage:
        copy.wait_recv()
    sum_x[:TILES] = (sum_core[x] + box_x[0]) + (box_x[1] + box_x[2])
    shared = TILES // PER_Z
    first_z = number[0]
    number[0] += 2 * (NZ - 1)

    def along_z(k, src, dst, i):
        return pltpu.make_async_remote_copy(
            src_ref=src, dst_ref=dst,
            send_sem=send_sem.at[first_z + k], recv_sem=recv_sem.at[first_z + k],
            device_id=across_z[i], device_id_type=MESH,
        )

    def part_copy(i):
        share = pl.ds(lax.rem(z + EIGHT[i], NZ) * PER_Z, PER_Z)
        return along_z(i, sum_x.at[share], box_z.at[i], i)

    share = pl.ds(z * PER_Z, PER_Z)

    def total_copy(i):
        own = full.at[y, x, core, share]
        return along_z(NZ - 1 + i, own, own, i)

    for i in range(NZ - 1):
        @pl.when(lax.rem(z + EIGHT[i], NZ) < shared)
        def _():
            part_copy(i).start()

    @pl.when(z < shared)
    def _():
        for i in range(NZ - 1):
            part_copy(i).wait_recv()
        total = sum_x[share]
        for i in range(NZ - 1):
            total = total + box_z[i]
        full[y, x, core, share] = total
        for i in range(NZ - 1):
            total_copy(i).start()

    for i in range(NZ - 1):
        @pl.when(lax.rem(z + NZ - EIGHT[i], NZ) < shared)
        def _():
            total_copy(i).wait_recv()

    def piece(y, x, core, half):
        return full.at[y, x, core, pl.ds(half * HALF, HALF)]

    def lay(y, x, core, half):
        base = ((y * NX + x) * NC + core) * 24
        for t in range(half * HALF, half * HALF + HALF):
            row = pl.multiple_of(base + t // 6 * 8, 8)
            col = t % 6 * 128
            whole[pl.ds(row, 8), col : col + 128] = full[y, x, core, t]

    def before(index, off, size):
        return lax.rem(index + size - off, size)

    steps = (0,) + FOUR

    one, two = piece(y, x, core, 0), piece(y, x, core, 1)
    one_x, two_y = spread(one, across_x), spread(two, across_y)
    one_y, two_x = [spread(one, across_y)], [spread(two, across_x)]
    siblings = [(spread(one, [sibling])[0], y, x, 0), (spread(two, [sibling])[0], y, x, 1)]
    lay(y, x, core, 0)
    lay(y, x, core, 1)
    for i in range(NX - 1):
        from_x = before(x, FOUR[i], NX)
        one_x[i].wait_recv()
        ref = piece(y, from_x, core, 0)
        one_y.append(spread(ref, across_y))
        siblings.append((spread(ref, [sibling])[0], y, from_x, 0))
        from_y = before(y, FOUR[i], NY)
        two_y[i].wait_recv()
        ref = piece(from_y, x, core, 1)
        two_x.append(spread(ref, across_x))
        siblings.append((spread(ref, [sibling])[0], from_y, x, 1))
        lay(y, from_x, core, 0)
        lay(from_y, x, core, 1)
    for n in range(NX):
        for i in range(NX - 1):
            at_x, at_y = before(x, steps[n], NX), before(y, FOUR[i], NY)
            one_y[n][i].wait_recv()
            siblings.append((spread(piece(at_y, at_x, core, 0), [sibling])[0], at_y, at_x, 0))
            lay(at_y, at_x, core, 0)
            at_x, at_y = before(x, FOUR[i], NX), before(y, steps[n], NY)
            two_x[n][i].wait_recv()
            siblings.append((spread(piece(at_y, at_x, core, 1), [sibling])[0], at_y, at_x, 1))
            lay(at_y, at_x, core, 1)
    for copy, at_y, at_x, half in siblings:
        copy.wait_recv()
        lay(at_y, at_x, 1 - core, half)

    rotation = newton(y, whole, a_high, a_low, h, h_high, h_low, t_high, t_low)
    rotation_ref[...] = rotation
    store_rotation = pltpu.make_async_copy(rotation_ref, rotation_hbm, local_sem.at[3])
    store_rotation.start()

    for copy in vectors_here:
        copy.wait_recv()
    rotated = dot(rotation.astype(BF16), vectors_all[...], NN)
    weights[:OWN, :] = rotated.astype(BF16)
    column = lax.broadcasted_iota(jnp.int32, (ROWS_K, K), 1)
    subspace = jnp.where(column < OWN, column // SUB, column - OWN)

    stage = []
    height = OWN_M * ROWS_K
    for n, (off, flip) in enumerate(((2, 0), (2, 1), (1, 0), (1, 1), (3, 0), (3, 1), (0, 1), (0, 0))):
        to_x, to_core = lax.rem(x + off, NX), lax.rem(core + flip, NC)
        chunk = pl.multiple_of((to_x * NC + to_core) * height, height)
        value = dot(onehot[pl.ds(chunk, height)], weights[...], NT)
        total = jnp.zeros((ROWS_K, K), F32)
        for m in range(OWN_M):
            total = jnp.where(subspace == m, value[m * ROWS_K : (m + 1) * ROWS_K], total)
        sums[n] = total
        if n < NX * NC - 1:
            stage.append(send(sums.at[n], box_one.at[n], device(to_x, z, to_core, y)))
    for copy in stage:
        copy.wait_recv()
    total = sums[NX * NC - 1]
    for i in range(len(stage)):
        total = total + box_one[i]
    for i in range(NZ):
        stage_two[i, 0:4] = total[i * 4 : i * 4 + 4]
    stage = [
        send(stage_two.at[lax.rem(z + EIGHT[i], NZ)], box_two.at[i], peer)
        for i, peer in enumerate(across_z)
    ]
    for copy in stage:
        copy.wait_recv()
    total = stage_two[z]
    for i in range(NZ - 1):
        total = total + box_two[i]
    refit_ref[...] = total
    for copy in sent:
        copy.wait_send()
    for i in range(NZ - 1):
        @pl.when(lax.rem(z + EIGHT[i], NZ) < shared)
        def _():
            part_copy(i).wait_send()
        @pl.when(z < shared)
        def _():
            total_copy(i).wait_send()
    store_rotation.wait()


def finish_kernel(rotation_ref, totals_ref, out_ref, refit_ref):
    out_ref[...] = rotation_ref[...]
    total = totals_ref[...]
    left, right = total[:, :128], total[:, 128:]
    lane = lax.broadcasted_iota(jnp.int32, (8, 128), 1)
    offset = OWN - 128
    count = jnp.take_along_axis(right, offset + lane // SUB, axis=1)
    refit_ref[:, :128] = (left / jnp.maximum(count, 1.0))[0:4]
    count = jnp.take_along_axis(right, offset + jnp.minimum((lane + 128) // SUB, OWN_M - 1), axis=1)
    refit_ref[:, 128:] = (right / jnp.maximum(count, 1.0))[0:4, :offset]


def per_device(vectors, codes, codebook):
    rows = vectors.shape[1]
    vmem = pl.BlockSpec(memory_space=pltpu.VMEM)
    anywhere = pl.BlockSpec(memory_space=pl.ANY)
    square = (D, D)
    copies = 9 + 3 + 4 + 3 + 7 + 7 + 12 + 2 + 24 + 24 + 7 + 7
    rotation, totals = pl.pallas_call(
        kernel,
        out_shape=(
            jax.ShapeDtypeStruct((OWN, D), F32),
            jax.ShapeDtypeStruct((8, K), F32),
        ),
        in_specs=[anywhere] * 3,
        out_specs=(anywhere, vmem),
        scratch_shapes=[
            pltpu.VMEM((OWN_M, rows), jnp.int32),
            pltpu.VMEM((OWN, D), F32),
            pltpu.VMEM((NY, OWN_M, rows), BF16),
            pltpu.VMEM((NY, 2, OWN // 2, K), BF16),
            pltpu.VMEM((D, rows), BF16),
            pltpu.VMEM((D, rows), BF16),
            pltpu.VMEM((NX, NC, TILES, 8, 128), F32),
            pltpu.VMEM((NX, TILES, 8, 128), F32),
            pltpu.VMEM((NX, TILES, 8, 128), F32),
            pltpu.VMEM((NX - 1, TILES, 8, 128), F32),
            pltpu.VMEM((PER_Z * NZ, 8, 128), F32),
            pltpu.VMEM((NZ - 1, PER_Z, 8, 128), F32),
            pltpu.VMEM((NY, NX, NC, PER_Z * NZ, 8, 128), F32),
            pltpu.VMEM(square, F32),
            pltpu.VMEM(square, BF16),
            pltpu.VMEM(square, BF16),
            pltpu.VMEM(square, F32),
            pltpu.VMEM(square, BF16),
            pltpu.VMEM(square, BF16),
            pltpu.VMEM(square, BF16),
            pltpu.VMEM(square, BF16),
            pltpu.VMEM((OWN_M * K, rows), BF16),
            pltpu.VMEM((K, rows), BF16),
            pltpu.VMEM((NX * NC, ROWS_K, K), F32),
            pltpu.VMEM((NX * NC - 1, ROWS_K, K), F32),
            pltpu.VMEM((NZ, 8, K), F32),
            pltpu.VMEM((NZ - 1, 8, K), F32),
            pltpu.SemaphoreType.DMA((copies,)),
            pltpu.SemaphoreType.DMA((copies,)),
            pltpu.SemaphoreType.DMA((4,)),
        ],
        compiler_params=pltpu.CompilerParams(
            collective_id=0, has_side_effects=True, vmem_limit_bytes=56 * 2**20
        ),
        name="rotate_and_refit",
    )(vectors, codes, codebook.T.reshape(2, OWN // 2, K))
    return pl.pallas_call(
        finish_kernel,
        out_shape=(
            jax.ShapeDtypeStruct((OWN, D), F32),
            jax.ShapeDtypeStruct((K // (NX * NZ * NC), OWN), F32),
        ),
        in_specs=[vmem, vmem],
        out_specs=(vmem, vmem),
        name="finish",
    )(rotation, totals)


def solution(mesh):
    placed = (P("dim", "dp"), P("dim", "dp"), P(None, "dim"))
    return jax.shard_map(
        per_device,
        mesh=mesh,
        in_specs=placed,
        out_specs=(P("dim", None), P("dp", "dim")),
        check_vma=False,
    )
```

```python
import jax
import jax.numpy as jnp
from jax import lax
from jax.experimental import pallas as pl
from jax.experimental.pallas import tpu as pltpu
from jax.sharding import PartitionSpec as P

NX, NZ, NC, NY = 4, 8, 2, 4
D, M, K = 768, 64, 256
SUB = D // M
OWN = D // NY
OWN_M = M // NY
TILES = 18
PER_Z = 3
HALF = TILES // 2
ROWS_K = K // NX // NC
FOUR = (2, 1, 3)
EIGHT = (4, 3, 5, 2, 6, 1, 7)
MESH = pl.DeviceIdType.MESH
F32, BF16 = jnp.float32, jnp.bfloat16
NT = (((1,), (1,)), ((), ()))
NN = (((1,), (0,)), ((), ()))


def dot(a, b, dims):
    return lax.dot_general(a, b, dims, preferred_element_type=F32)


def split(value):
    high = value.astype(BF16)
    return high, (value - high.astype(F32)).astype(BF16)


def product(a_high, a_low, b_high, b_low, dims):
    return dot(a_high, b_high, dims) + (dot(a_high, b_low, dims) + dot(a_low, b_high, dims))


def position():
    dp = lax.axis_index("dp")
    y = lax.axis_index("dim")
    core = lax.rem(dp, NC)
    z = lax.rem(dp // NC, NZ)
    x = dp // (NC * NZ)
    return x, z, core, y


def device(x, z, core, y):
    return ((x * NZ + z) * NC + core, y)


def own_rows(y):
    return pl.ds(pl.multiple_of(y * OWN, 64), OWN)


def decode(codes_all, book_all, decoded, y, half):
    group = OWN_M // 2
    height = group * SUB
    rows = decoded.shape[1]
    which = lax.broadcasted_iota(jnp.int32, (height, 128), 0) // SUB
    book = book_all[y, half].astype(F32)
    low, high = book[:, :128], book[:, 128:]
    base = pl.multiple_of(y * OWN + half * height, 32)
    for block in range(rows // 128):
        cols = pl.ds(block * 128, 128)
        both = codes_all[y, :, cols].astype(F32).astype(jnp.int32)
        lines = jnp.where(half == 0, both[:group], both[group:])
        index = jnp.broadcast_to(lines[0:1], (height, 128))
        for s in range(1, group):
            line = jnp.broadcast_to(lines[s : s + 1], (height, 128))
            index = jnp.where(which == s, line, index)
        lane = index & 127
        picked = jnp.where(
            index >= 128,
            jnp.take_along_axis(high, lane, axis=1),
            jnp.take_along_axis(low, lane, axis=1),
        )
        decoded[pl.ds(base, height), cols] = picked.astype(BF16)


def newton(y, whole, a_high, a_low, h, h_high, h_low, t_high, t_low):
    squares = [jnp.zeros((8, 128), F32)] * 12
    for s in range(D // 8):
        for j in range(D // 128):
            tile = whole[s * 8 : s * 8 + 8, j * 128 : j * 128 + 128]
            n = s % 2 * 6 + j
            squares[n] = squares[n] + tile * tile
    energy = jnp.sum(sum(squares[1:], squares[0]))
    scale = 1.0 / energy
    side = 256
    count = D // side

    def cut(i):
        return slice(i * side, i * side + side)

    for i in range(count):
        a_high[cut(i)], a_low[cut(i)] = split(whole[cut(i)])

    start = pl.multiple_of(y * OWN - 64 * lax.rem(y, 2), 128)
    own = whole[:, pl.ds(start, 256)]
    own = jnp.where(lax.rem(y, 2) == 1, pltpu.roll(own, 192, 1), own)
    own = own.T[:OWN] / jnp.sqrt(energy)

    upper = [(i, j) for i in range(count) for j in range(i, count)]

    def put(full, high, low, i, j, value):
        full[cut(i), cut(j)] = value
        high[cut(i), cut(j)], low[cut(i), cut(j)] = split(value)
        if i != j:
            high[cut(j), cut(i)], low[cut(j), cut(i)] = split(value.T)

    def times_h(value):
        high, low = split(value)
        both = dot(jnp.concatenate([high, low], axis=0), h_high[...], NN)
        return both[:OWN] + (both[OWN:] + dot(high, h_low[...], NN))

    for i, j in upper:
        value = product(a_high[cut(i)], a_low[cut(i)], a_high[cut(j)], a_low[cut(j)], NT)
        put(h, h_high, h_low, i, j, value * scale)
    for step in range(2):
        own = 1.5 * own - 0.5 * times_h(own)
        for i, j in upper:
            value = product(h_high[cut(i)], h_low[cut(i)], h_high[:, cut(j)], h_low[:, cut(j)], NN)
            put(whole, t_high, t_low, i, j, 1.5 * h[cut(i), cut(j)] - 0.5 * value)
        for i, j in upper:
            value = product(t_high[cut(i)], t_low[cut(i)], h_high[:, cut(j)], h_low[:, cut(j)], NN)
            h[cut(i), cut(j)] = 1.5 * whole[cut(i), cut(j)] - 0.5 * value
        for i, j in upper:
            put(h, h_high, h_low, i, j, h[cut(i), cut(j)])
    own = 1.5 * own - 0.5 * times_h(own)
    last = times_h(own)
    for _ in range(2):
        last = 1.5 * last - 0.5 * times_h(last)
    return 1.5 * own - 0.5 * last


def kernel(
    vectors_hbm, codes_hbm, book_hbm, rotation_hbm, refit_ref,
    codes_ref, rotation_ref, codes_all, book_all, vectors_all, decoded, part, box_core, sum_core, box_x, sum_x, box_z,
    full, whole, a_high, a_low, h, h_high, h_low, t_high, t_low,
    onehot, weights, sums, box_one, stage_two, box_two, send_sem, recv_sem, local_sem,
):
    x, z, core, y = position()
    rows = vectors_all.shape[1]
    sibling = device(x, z, 1 - core, y)
    across_x = [device(lax.rem(x + off, NX), z, core, y) for off in FOUR]
    across_z = [device(x, lax.rem(z + off, NZ), core, y) for off in EIGHT]
    across_y = [device(x, z, core, lax.rem(y + off, NY)) for off in FOUR]
    other_x = [
        device(lax.rem(x + off, NX), z, 1 - core, y) for off in range(1, NX)
    ]
    sent = []
    number = [0]

    def send(src, dst, peer):
        k = number[0]
        number[0] += 1
        copy = pltpu.make_async_remote_copy(
            src_ref=src, dst_ref=dst, send_sem=send_sem.at[k], recv_sem=recv_sem.at[k],
            device_id=peer, device_id_type=MESH,
        )
        copy.start()
        sent.append(copy)
        return copy

    def spread(ref, peers):
        return [send(ref, ref, peer) for peer in peers]

    barrier = pltpu.get_barrier_semaphore()
    peers = across_z + other_x + across_x + across_y + [sibling]
    for peer in peers:
        pl.semaphore_signal(barrier, inc=1, device_id=peer, device_id_type=MESH)
    mine = vectors_all.at[own_rows(y), :]
    load_codes = pltpu.make_async_copy(codes_hbm, codes_ref, local_sem.at[0])
    load_book = pltpu.make_async_copy(book_hbm, book_all.at[y], local_sem.at[1])
    load_vectors = pltpu.make_async_copy(vectors_hbm, mine, local_sem.at[2])
    for copy in (load_codes, load_book, load_vectors):
        copy.start()
    stage_two[...] = jnp.zeros((NZ, 8, K), F32)
    weights[OWN:, :] = jnp.where(
        lax.broadcasted_iota(jnp.int32, (K - OWN, rows), 0) < OWN_M, 1.0, 0.0
    ).astype(BF16)
    load_codes.wait()
    codes_all[y] = codes_ref[...].astype(F32).astype(BF16)
    load_book.wait()
    load_vectors.wait()
    pl.semaphore_wait(barrier, len(peers))

    arrivals = []
    for peer in across_y:
        arrivals += spread(codes_all.at[y], [peer]) + spread(book_all.at[y, core], [peer])
    decode(codes_all, book_all, decoded, y, core)
    decode(codes_all, book_all, decoded, y, 1 - core)
    sources = [lax.rem(y + NY - off, NY) for off in FOUR]
    passed = []
    for i, source in enumerate(sources):
        arrivals[2 * i].wait_recv()
        arrivals[2 * i + 1].wait_recv()
        passed += spread(book_all.at[source, core], [sibling])
        decode(codes_all, book_all, decoded, source, core)
    for i, source in enumerate(sources):
        passed[i].wait_recv()
        decode(codes_all, book_all, decoded, source, 1 - core)
    vectors_here = spread(mine, across_y)

    value = dot(vectors_all[own_rows(y), :], decoded[...], NT)
    for pair in range(NX * NC):
        for t in range(TILES):
            i, j = pair * 3 + t // 6, t % 6
            part[pair // NC, pair % NC, t] = value[i * 8 : i * 8 + 8, j * 128 : j * 128 + 128]

    order = [lax.rem(x + off, NX) for off in FOUR + (0,)]
    first = [send(part.at[i, 1 - core], box_core.at[i], sibling) for i in order]
    stage = []
    for n, copy in enumerate(first):
        i = order[n]
        copy.wait_recv()
        sum_core[i] = part[i, core] + box_core[i]
        if n < NX - 1:
            stage.append(send(sum_core.at[i], box_x.at[n], across_x[n]))
    place = lax.broadcasted_iota(jnp.int32, (ROWS_K, rows), 0)
    level = place // 4 * 8 + place % 4
    for m in range(OWN_M):
        code = jnp.broadcast_to(codes_ref[m : m + 1, :], (ROWS_K, rows))
        for chunk in range(NX * NC):
            at = (chunk * OWN_M + m) * ROWS_K
            same = level == code - (chunk // NC * 64 + chunk % NC * 4)
            onehot[at : at + ROWS_K] = jnp.where(same, 1.0, 0.0).astype(BF16)
    for copy in stage:
        copy.wait_recv()
    sum_x[:TILES] = (sum_core[x] + box_x[0]) + (box_x[1] + box_x[2])
    shared = TILES // PER_Z
    first_z = number[0]
    number[0] += 2 * (NZ - 1)

    def along_z(k, src, dst, i):
        return pltpu.make_async_remote_copy(
            src_ref=src, dst_ref=dst,
            send_sem=send_sem.at[first_z + k], recv_sem=recv_sem.at[first_z + k],
            device_id=across_z[i], device_id_type=MESH,
        )

    def part_copy(i):
        share = pl.ds(lax.rem(z + EIGHT[i], NZ) * PER_Z, PER_Z)
        return along_z(i, sum_x.at[share], box_z.at[i], i)

    share = pl.ds(z * PER_Z, PER_Z)

    def total_copy(i):
        own = full.at[y, x, core, share]
        return along_z(NZ - 1 + i, own, own, i)

    for i in range(NZ - 1):
        @pl.when(lax.rem(z + EIGHT[i], NZ) < shared)
        def _():
            part_copy(i).start()

    @pl.when(z < shared)
    def _():
        for i in range(NZ - 1):
            part_copy(i).wait_recv()
        total = sum_x[share]
        for i in range(NZ - 1):
            total = total + box_z[i]
        full[y, x, core, share] = total
        for i in range(NZ - 1):
            total_copy(i).start()

    def await_half(half):
        for i in range(NZ - 1):
            @pl.when(lax.rem(z + NZ - EIGHT[i], NZ) // (shared // 2) == half)
            def _():
                total_copy(i).wait_recv()

    def piece(y, x, core, half):
        return full.at[y, x, core, pl.ds(half * HALF, HALF)]

    def lay(y, x, core, half):
        base = ((y * NX + x) * NC + core) * 24
        for t in range(half * HALF, half * HALF + HALF):
            row = pl.multiple_of(base + t // 6 * 8, 8)
            col = t % 6 * 128
            whole[pl.ds(row, 8), col : col + 128] = full[y, x, core, t]

    def before(index, off, size):
        return lax.rem(index + size - off, size)

    steps = (0,) + FOUR

    one, two = piece(y, x, core, 0), piece(y, x, core, 1)
    await_half(0)
    one_x = spread(one, across_x)
    await_half(1)
    two_y = spread(two, across_y)
    one_y, two_x = [spread(one, across_y)], [spread(two, across_x)]
    siblings = [(spread(one, [sibling])[0], y, x, 0), (spread(two, [sibling])[0], y, x, 1)]
    lay(y, x, core, 0)
    lay(y, x, core, 1)
    for i in range(NX - 1):
        from_x = before(x, FOUR[i], NX)
        one_x[i].wait_recv()
        ref = piece(y, from_x, core, 0)
        one_y.append(spread(ref, across_y))
        siblings.append((spread(ref, [sibling])[0], y, from_x, 0))
        from_y = before(y, FOUR[i], NY)
        two_y[i].wait_recv()
        ref = piece(from_y, x, core, 1)
        two_x.append(spread(ref, across_x))
        siblings.append((spread(ref, [sibling])[0], from_y, x, 1))
        lay(y, from_x, core, 0)
        lay(from_y, x, core, 1)
    for n in range(NX):
        for i in range(NX - 1):
            at_x, at_y = before(x, steps[n], NX), before(y, FOUR[i], NY)
            one_y[n][i].wait_recv()
            siblings.append((spread(piece(at_y, at_x, core, 0), [sibling])[0], at_y, at_x, 0))
            lay(at_y, at_x, core, 0)
            at_x, at_y = before(x, FOUR[i], NX), before(y, steps[n], NY)
            two_x[n][i].wait_recv()
            siblings.append((spread(piece(at_y, at_x, core, 1), [sibling])[0], at_y, at_x, 1))
            lay(at_y, at_x, core, 1)
    for copy, at_y, at_x, half in siblings:
        copy.wait_recv()
        lay(at_y, at_x, 1 - core, half)

    rotation = newton(y, whole, a_high, a_low, h, h_high, h_low, t_high, t_low)
    rotation_ref[...] = rotation
    store_rotation = pltpu.make_async_copy(rotation_ref, rotation_hbm, local_sem.at[3])
    store_rotation.start()

    for copy in vectors_here:
        copy.wait_recv()
    rotated = dot(rotation.astype(BF16), vectors_all[...], NN)
    weights[:OWN, :] = rotated.astype(BF16)
    column = lax.broadcasted_iota(jnp.int32, (ROWS_K, K), 1)
    subspace = jnp.where(column < OWN, column // SUB, column - OWN)

    stage = []
    height = OWN_M * ROWS_K
    for n, (off, flip) in enumerate(((2, 0), (2, 1), (1, 0), (1, 1), (3, 0), (3, 1), (0, 1), (0, 0))):
        to_x, to_core = lax.rem(x + off, NX), lax.rem(core + flip, NC)
        chunk = pl.multiple_of((to_x * NC + to_core) * height, height)
        value = dot(onehot[pl.ds(chunk, height)], weights[...], NT)
        total = jnp.zeros((ROWS_K, K), F32)
        for m in range(OWN_M):
            total = jnp.where(subspace == m, value[m * ROWS_K : (m + 1) * ROWS_K], total)
        sums[n] = total
        if n < NX * NC - 1:
            stage.append(send(sums.at[n], box_one.at[n], device(to_x, z, to_core, y)))
    for copy in stage:
        copy.wait_recv()
    total = sums[NX * NC - 1]
    for i in range(len(stage)):
        total = total + box_one[i]
    for i in range(NZ):
        stage_two[i, 0:4] = total[i * 4 : i * 4 + 4]
    stage = [
        send(stage_two.at[lax.rem(z + EIGHT[i], NZ)], box_two.at[i], peer)
        for i, peer in enumerate(across_z)
    ]
    for copy in stage:
        copy.wait_recv()
    total = stage_two[z]
    for i in range(NZ - 1):
        total = total + box_two[i]
    refit_ref[...] = total
    for copy in sent:
        copy.wait_send()
    for i in range(NZ - 1):
        @pl.when(lax.rem(z + EIGHT[i], NZ) < shared)
        def _():
            part_copy(i).wait_send()
        @pl.when(z < shared)
        def _():
            total_copy(i).wait_send()
    store_rotation.wait()


def finish_kernel(rotation_ref, totals_ref, out_ref, refit_ref):
    out_ref[...] = rotation_ref[...]
    total = totals_ref[...]
    left, right = total[:, :128], total[:, 128:]
    lane = lax.broadcasted_iota(jnp.int32, (8, 128), 1)
    offset = OWN - 128
    count = jnp.take_along_axis(right, offset + lane // SUB, axis=1)
    refit_ref[:, :128] = (left / jnp.maximum(count, 1.0))[0:4]
    count = jnp.take_along_axis(right, offset + jnp.minimum((lane + 128) // SUB, OWN_M - 1), axis=1)
    refit_ref[:, 128:] = (right / jnp.maximum(count, 1.0))[0:4, :offset]


def per_device(vectors, codes, codebook):
    rows = vectors.shape[1]
    vmem = pl.BlockSpec(memory_space=pltpu.VMEM)
    anywhere = pl.BlockSpec(memory_space=pl.ANY)
    square = (D, D)
    copies = 9 + 3 + 4 + 3 + 7 + 7 + 12 + 2 + 24 + 24 + 7 + 7
    rotation, totals = pl.pallas_call(
        kernel,
        out_shape=(
            jax.ShapeDtypeStruct((OWN, D), F32),
            jax.ShapeDtypeStruct((8, K), F32),
        ),
        in_specs=[anywhere] * 3,
        out_specs=(anywhere, vmem),
        scratch_shapes=[
            pltpu.VMEM((OWN_M, rows), jnp.int32),
            pltpu.VMEM((OWN, D), F32),
            pltpu.VMEM((NY, OWN_M, rows), BF16),
            pltpu.VMEM((NY, 2, OWN // 2, K), BF16),
            pltpu.VMEM((D, rows), BF16),
            pltpu.VMEM((D, rows), BF16),
            pltpu.VMEM((NX, NC, TILES, 8, 128), F32),
            pltpu.VMEM((NX, TILES, 8, 128), F32),
            pltpu.VMEM((NX, TILES, 8, 128), F32),
            pltpu.VMEM((NX - 1, TILES, 8, 128), F32),
            pltpu.VMEM((PER_Z * NZ, 8, 128), F32),
            pltpu.VMEM((NZ - 1, PER_Z, 8, 128), F32),
            pltpu.VMEM((NY, NX, NC, PER_Z * NZ, 8, 128), F32),
            pltpu.VMEM(square, F32),
            pltpu.VMEM(square, BF16),
            pltpu.VMEM(square, BF16),
            pltpu.VMEM(square, F32),
            pltpu.VMEM(square, BF16),
            pltpu.VMEM(square, BF16),
            pltpu.VMEM(square, BF16),
            pltpu.VMEM(square, BF16),
            pltpu.VMEM((OWN_M * K, rows), BF16),
            pltpu.VMEM((K, rows), BF16),
            pltpu.VMEM((NX * NC, ROWS_K, K), F32),
            pltpu.VMEM((NX * NC - 1, ROWS_K, K), F32),
            pltpu.VMEM((NZ, 8, K), F32),
            pltpu.VMEM((NZ - 1, 8, K), F32),
            pltpu.SemaphoreType.DMA((copies,)),
            pltpu.SemaphoreType.DMA((copies,)),
            pltpu.SemaphoreType.DMA((4,)),
        ],
        compiler_params=pltpu.CompilerParams(
            collective_id=0, has_side_effects=True, vmem_limit_bytes=56 * 2**20
        ),
        name="rotate_and_refit",
    )(vectors, codes, codebook.T.reshape(2, OWN // 2, K))
    return pl.pallas_call(
        finish_kernel,
        out_shape=(
            jax.ShapeDtypeStruct((OWN, D), F32),
            jax.ShapeDtypeStruct((K // (NX * NZ * NC), OWN), F32),
        ),
        in_specs=[vmem, vmem],
        out_specs=(vmem, vmem),
        name="finish",
    )(rotation, totals)


def solution(mesh):
    placed = (P("dim", "dp"), P("dim", "dp"), P(None, "dim"))
    return jax.shard_map(
        per_device,
        mesh=mesh,
        in_specs=placed,
        out_specs=(P("dim", None), P("dp", "dim")),
        check_vma=False,
    )
```

```python
import jax
import jax.numpy as jnp
from jax import lax
from jax.experimental import pallas as pl
from jax.experimental.pallas import tpu as pltpu
from jax.sharding import PartitionSpec as P

NX, NZ, NC, NY = 4, 8, 2, 4
D, M, K = 768, 64, 256
SUB = D // M
OWN = D // NY
OWN_M = M // NY
TILES = 18
PER_Z = 3
HALF = TILES // 2
ROWS_K = K // NX // NC
FOUR = (2, 1, 3)
EIGHT = (4, 3, 5, 2, 6, 1, 7)
MESH = pl.DeviceIdType.MESH
F32, BF16 = jnp.float32, jnp.bfloat16
NT = (((1,), (1,)), ((), ()))
NN = (((1,), (0,)), ((), ()))


def dot(a, b, dims):
    return lax.dot_general(a, b, dims, preferred_element_type=F32)


def split(value):
    high = value.astype(BF16)
    return high, (value - high.astype(F32)).astype(BF16)


def product(a_high, a_low, b_high, b_low, dims):
    return dot(a_high, b_high, dims) + (dot(a_high, b_low, dims) + dot(a_low, b_high, dims))


def position():
    dp = lax.axis_index("dp")
    y = lax.axis_index("dim")
    core = lax.rem(dp, NC)
    z = lax.rem(dp // NC, NZ)
    x = dp // (NC * NZ)
    return x, z, core, y


def device(x, z, core, y):
    return ((x * NZ + z) * NC + core, y)


def own_rows(y):
    return pl.ds(pl.multiple_of(y * OWN, 64), OWN)


def decode(codes_all, book_all, decoded, y, half):
    group = OWN_M // 2
    height = group * SUB
    rows = decoded.shape[1]
    which = lax.broadcasted_iota(jnp.int32, (height, 128), 0) // SUB
    book = book_all[y, half].astype(F32)
    low, high = book[:, :128], book[:, 128:]
    base = pl.multiple_of(y * OWN + half * height, 32)
    for block in range(rows // 128):
        cols = pl.ds(block * 128, 128)
        both = codes_all[y, :, cols].astype(F32).astype(jnp.int32)
        lines = jnp.where(half == 0, both[:group], both[group:])
        index = jnp.broadcast_to(lines[0:1], (height, 128))
        for s in range(1, group):
            line = jnp.broadcast_to(lines[s : s + 1], (height, 128))
            index = jnp.where(which == s, line, index)
        lane = index & 127
        picked = jnp.where(
            index >= 128,
            jnp.take_along_axis(high, lane, axis=1),
            jnp.take_along_axis(low, lane, axis=1),
        )
        decoded[pl.ds(base, height), cols] = picked.astype(BF16)


def newton(y, whole, a_high, a_low, h, h_high, h_low, t_high, t_low):
    squares = [jnp.zeros((8, 128), F32)] * 12
    for s in range(D // 8):
        for j in range(D // 128):
            tile = whole[s * 8 : s * 8 + 8, j * 128 : j * 128 + 128]
            n = s % 2 * 6 + j
            squares[n] = squares[n] + tile * tile
    energy = jnp.sum(sum(squares[1:], squares[0]))
    scale = 1.0 / energy
    side = 256
    count = D // side

    def cut(i):
        return slice(i * side, i * side + side)

    for i in range(count):
        a_high[cut(i)], a_low[cut(i)] = split(whole[cut(i)])

    start = pl.multiple_of(y * OWN - 64 * lax.rem(y, 2), 128)
    own = whole[:, pl.ds(start, 256)]
    own = jnp.where(lax.rem(y, 2) == 1, pltpu.roll(own, 192, 1), own)
    own = own.T[:OWN] / jnp.sqrt(energy)

    upper = [(i, j) for i in range(count) for j in range(i, count)]

    def put(full, high, low, i, j, value):
        full[cut(i), cut(j)] = value
        high[cut(i), cut(j)], low[cut(i), cut(j)] = split(value)
        if i != j:
            high[cut(j), cut(i)], low[cut(j), cut(i)] = split(value.T)

    def times_h(value):
        high, low = split(value)
        both = dot(jnp.concatenate([high, low], axis=0), h_high[...], NN)
        return both[:OWN] + (both[OWN:] + dot(high, h_low[...], NN))

    for i, j in upper:
        value = product(a_high[cut(i)], a_low[cut(i)], a_high[cut(j)], a_low[cut(j)], NT)
        put(h, h_high, h_low, i, j, value * scale)
    for step in range(2):
        own = 1.5 * own - 0.5 * times_h(own)
        for i, j in upper:
            value = product(h_high[cut(i)], h_low[cut(i)], h_high[:, cut(j)], h_low[:, cut(j)], NN)
            put(whole, t_high, t_low, i, j, 1.5 * h[cut(i), cut(j)] - 0.5 * value)
        for i, j in upper:
            value = product(t_high[cut(i)], t_low[cut(i)], h_high[:, cut(j)], h_low[:, cut(j)], NN)
            h[cut(i), cut(j)] = 1.5 * whole[cut(i), cut(j)] - 0.5 * value
        for i, j in upper:
            put(h, h_high, h_low, i, j, h[cut(i), cut(j)])
    own = 1.5 * own - 0.5 * times_h(own)
    last = times_h(own)
    for _ in range(2):
        last = 1.5 * last - 0.5 * times_h(last)
    return 1.5 * own - 0.5 * last


def kernel(
    vectors_hbm, codes_hbm, book_hbm, rotation_hbm, refit_ref,
    codes_ref, rotation_ref, codes_all, book_all, vectors_all, decoded, part, box_core, sum_core, box_x, sum_x, box_z,
    full, whole, a_high, a_low, h, h_high, h_low, t_high, t_low,
    onehot, weights, sums, box_one, stage_two, box_two, send_sem, recv_sem, local_sem,
):
    x, z, core, y = position()
    rows = vectors_all.shape[1]
    sibling = device(x, z, 1 - core, y)
    across_x = [device(lax.rem(x + off, NX), z, core, y) for off in FOUR]
    across_z = [device(x, lax.rem(z + off, NZ), core, y) for off in EIGHT]
    across_y = [device(x, z, core, lax.rem(y + off, NY)) for off in FOUR]
    other_x = [
        device(lax.rem(x + off, NX), z, 1 - core, y) for off in range(1, NX)
    ]
    sent = []
    number = [0]

    def send(src, dst, peer):
        k = number[0]
        number[0] += 1
        copy = pltpu.make_async_remote_copy(
            src_ref=src, dst_ref=dst, send_sem=send_sem.at[k], recv_sem=recv_sem.at[k],
            device_id=peer, device_id_type=MESH,
        )
        copy.start()
        sent.append(copy)
        return copy

    def spread(ref, peers):
        return [send(ref, ref, peer) for peer in peers]

    barrier = pltpu.get_barrier_semaphore()
    peers = across_z + other_x + across_x + across_y + [sibling]
    for peer in peers:
        pl.semaphore_signal(barrier, inc=1, device_id=peer, device_id_type=MESH)
    mine = vectors_all.at[own_rows(y), :]
    load_codes = pltpu.make_async_copy(codes_hbm, codes_ref, local_sem.at[0])
    load_book = pltpu.make_async_copy(book_hbm, book_all.at[y], local_sem.at[1])
    load_vectors = pltpu.make_async_copy(vectors_hbm, mine, local_sem.at[2])
    for copy in (load_codes, load_book, load_vectors):
        copy.start()
    stage_two[...] = jnp.zeros((NZ, 8, K), F32)
    weights[OWN:, :] = jnp.where(
        lax.broadcasted_iota(jnp.int32, (K - OWN, rows), 0) < OWN_M, 1.0, 0.0
    ).astype(BF16)
    load_codes.wait()
    codes_all[y] = codes_ref[...].astype(F32).astype(BF16)
    load_book.wait()
    load_vectors.wait()
    pl.semaphore_wait(barrier, len(peers))

    arrivals = []
    for peer in across_y:
        arrivals += spread(codes_all.at[y], [peer]) + spread(book_all.at[y, core], [peer])
    decode(codes_all, book_all, decoded, y, core)
    decode(codes_all, book_all, decoded, y, 1 - core)
    sources = [lax.rem(y + NY - off, NY) for off in FOUR]
    passed = []
    for i, source in enumerate(sources):
        arrivals[2 * i].wait_recv()
        arrivals[2 * i + 1].wait_recv()
        passed += spread(book_all.at[source, core], [sibling])
        decode(codes_all, book_all, decoded, source, core)
    for i, source in enumerate(sources):
        passed[i].wait_recv()
        decode(codes_all, book_all, decoded, source, 1 - core)
    vectors_here = spread(mine, across_y)

    value = dot(vectors_all[own_rows(y), :], decoded[...], NT)
    for pair in range(NX * NC):
        for t in range(TILES):
            i, j = pair * 3 + t // 6, t % 6
            part[pair // NC, pair % NC, t] = value[i * 8 : i * 8 + 8, j * 128 : j * 128 + 128]

    order = [lax.rem(x + off, NX) for off in FOUR + (0,)]
    first = [send(part.at[i, 1 - core], box_core.at[i], sibling) for i in order]
    stage = []
    for n, copy in enumerate(first):
        i = order[n]
        copy.wait_recv()
        sum_core[i] = part[i, core] + box_core[i]
        if n < NX - 1:
            stage.append(send(sum_core.at[i], box_x.at[n], across_x[n]))
    place = lax.broadcasted_iota(jnp.int32, (ROWS_K, rows), 0)
    level = place // 4 * 8 + place % 4
    for m in range(OWN_M):
        code = jnp.broadcast_to(codes_ref[m : m + 1, :], (ROWS_K, rows))
        for chunk in range(NX * NC):
            at = (chunk * OWN_M + m) * ROWS_K
            same = level == code - (chunk // NC * 64 + chunk % NC * 4)
            onehot[at : at + ROWS_K] = jnp.where(same, 1.0, 0.0).astype(BF16)
    for copy in stage:
        copy.wait_recv()
    sum_x[:TILES] = (sum_core[x] + box_x[0]) + (box_x[1] + box_x[2])
    shared = TILES // PER_Z
    first_z = number[0]
    number[0] += 2 * (NZ - 1)

    def along_z(k, src, dst, i):
        return pltpu.make_async_remote_copy(
            src_ref=src, dst_ref=dst,
            send_sem=send_sem.at[first_z + k], recv_sem=recv_sem.at[first_z + k],
            device_id=across_z[i], device_id_type=MESH,
        )

    def part_copy(i):
        share = pl.ds(lax.rem(z + EIGHT[i], NZ) * PER_Z, PER_Z)
        return along_z(i, sum_x.at[share], box_z.at[i], i)

    share = pl.ds(z * PER_Z, PER_Z)

    def total_copy(i):
        own = full.at[y, x, core, share]
        return along_z(NZ - 1 + i, own, own, i)

    for i in range(NZ - 1):
        @pl.when(lax.rem(z + EIGHT[i], NZ) < shared)
        def _():
            part_copy(i).start()

    @pl.when(z < shared)
    def _():
        for i in range(NZ - 1):
            part_copy(i).wait_recv()
        total = sum_x[share]
        for i in range(NZ - 1):
            total = total + box_z[i]
        full[y, x, core, share] = total
        for i in range(NZ - 1):
            total_copy(i).start()

    def await_half(half):
        for i in range(NZ - 1):
            @pl.when(lax.rem(z + NZ - EIGHT[i], NZ) // (shared // 2) == half)
            def _():
                total_copy(i).wait_recv()

    def piece(y, x, core, half):
        return full.at[y, x, core, pl.ds(half * HALF, HALF)]

    def lay(y, x, core, half):
        base = ((y * NX + x) * NC + core) * 24
        for t in range(half * HALF, half * HALF + HALF):
            row = pl.multiple_of(base + t // 6 * 8, 8)
            col = t % 6 * 128
            whole[pl.ds(row, 8), col : col + 128] = full[y, x, core, t]

    def before(index, off, size):
        return lax.rem(index + size - off, size)

    steps = (0,) + FOUR

    one, two = piece(y, x, core, 0), piece(y, x, core, 1)
    await_half(0)
    one_x = spread(one, across_x)
    siblings = [(spread(one, [sibling])[0], y, x, 0)]
    lay(y, x, core, 0)
    await_half(1)
    two_y = spread(two, across_y)
    one_y, two_x = [spread(one, across_y)], [spread(two, across_x)]
    siblings.append((spread(two, [sibling])[0], y, x, 1))
    lay(y, x, core, 1)
    for i in range(NX - 1):
        from_x = before(x, FOUR[i], NX)
        one_x[i].wait_recv()
        ref = piece(y, from_x, core, 0)
        one_y.append(spread(ref, across_y))
        siblings.append((spread(ref, [sibling])[0], y, from_x, 0))
        from_y = before(y, FOUR[i], NY)
        two_y[i].wait_recv()
        ref = piece(from_y, x, core, 1)
        two_x.append(spread(ref, across_x))
        siblings.append((spread(ref, [sibling])[0], from_y, x, 1))
        lay(y, from_x, core, 0)
        lay(from_y, x, core, 1)
    for n in range(NX):
        for i in range(NX - 1):
            at_x, at_y = before(x, steps[n], NX), before(y, FOUR[i], NY)
            one_y[n][i].wait_recv()
            siblings.append((spread(piece(at_y, at_x, core, 0), [sibling])[0], at_y, at_x, 0))
            lay(at_y, at_x, core, 0)
            at_x, at_y = before(x, FOUR[i], NX), before(y, steps[n], NY)
            two_x[n][i].wait_recv()
            siblings.append((spread(piece(at_y, at_x, core, 1), [sibling])[0], at_y, at_x, 1))
            lay(at_y, at_x, core, 1)
    for copy, at_y, at_x, half in siblings:
        copy.wait_recv()
        lay(at_y, at_x, 1 - core, half)

    rotation = newton(y, whole, a_high, a_low, h, h_high, h_low, t_high, t_low)
    rotation_ref[...] = rotation
    store_rotation = pltpu.make_async_copy(rotation_ref, rotation_hbm, local_sem.at[3])
    store_rotation.start()

    for copy in vectors_here:
        copy.wait_recv()
    rotated = dot(rotation.astype(BF16), vectors_all[...], NN)
    weights[:OWN, :] = rotated.astype(BF16)
    column = lax.broadcasted_iota(jnp.int32, (ROWS_K, K), 1)
    subspace = jnp.where(column < OWN, column // SUB, column - OWN)

    stage = []
    height = OWN_M * ROWS_K
    for n, (off, flip) in enumerate(((2, 0), (2, 1), (1, 0), (1, 1), (3, 0), (3, 1), (0, 1), (0, 0))):
        to_x, to_core = lax.rem(x + off, NX), lax.rem(core + flip, NC)
        chunk = pl.multiple_of((to_x * NC + to_core) * height, height)
        value = dot(onehot[pl.ds(chunk, height)], weights[...], NT)
        total = jnp.zeros((ROWS_K, K), F32)
        for m in range(OWN_M):
            total = jnp.where(subspace == m, value[m * ROWS_K : (m + 1) * ROWS_K], total)
        sums[n] = total
        if n < NX * NC - 1:
            stage.append(send(sums.at[n], box_one.at[n], device(to_x, z, to_core, y)))
    for copy in stage:
        copy.wait_recv()
    total = sums[NX * NC - 1]
    for i in range(len(stage)):
        total = total + box_one[i]
    for i in range(NZ):
        stage_two[i, 0:4] = total[i * 4 : i * 4 + 4]
    stage = [
        send(stage_two.at[lax.rem(z + EIGHT[i], NZ)], box_two.at[i], peer)
        for i, peer in enumerate(across_z)
    ]
    for copy in stage:
        copy.wait_recv()
    total = stage_two[z]
    for i in range(NZ - 1):
        total = total + box_two[i]
    refit_ref[...] = total
    for copy in sent:
        copy.wait_send()
    for i in range(NZ - 1):
        @pl.when(lax.rem(z + EIGHT[i], NZ) < shared)
        def _():
            part_copy(i).wait_send()
        @pl.when(z < shared)
        def _():
            total_copy(i).wait_send()
    store_rotation.wait()


def finish_kernel(rotation_ref, totals_ref, out_ref, refit_ref):
    out_ref[...] = rotation_ref[...]
    total = totals_ref[...]
    left, right = total[:, :128], total[:, 128:]
    lane = lax.broadcasted_iota(jnp.int32, (8, 128), 1)
    offset = OWN - 128
    count = jnp.take_along_axis(right, offset + lane // SUB, axis=1)
    refit_ref[:, :128] = (left / jnp.maximum(count, 1.0))[0:4]
    count = jnp.take_along_axis(right, offset + jnp.minimum((lane + 128) // SUB, OWN_M - 1), axis=1)
    refit_ref[:, 128:] = (right / jnp.maximum(count, 1.0))[0:4, :offset]


def per_device(vectors, codes, codebook):
    rows = vectors.shape[1]
    vmem = pl.BlockSpec(memory_space=pltpu.VMEM)
    anywhere = pl.BlockSpec(memory_space=pl.ANY)
    square = (D, D)
    copies = 9 + 3 + 4 + 3 + 7 + 7 + 12 + 2 + 24 + 24 + 7 + 7
    rotation, totals = pl.pallas_call(
        kernel,
        out_shape=(
            jax.ShapeDtypeStruct((OWN, D), F32),
            jax.ShapeDtypeStruct((8, K), F32),
        ),
        in_specs=[anywhere] * 3,
        out_specs=(anywhere, vmem),
        scratch_shapes=[
            pltpu.VMEM((OWN_M, rows), jnp.int32),
            pltpu.VMEM((OWN, D), F32),
            pltpu.VMEM((NY, OWN_M, rows), BF16),
            pltpu.VMEM((NY, 2, OWN // 2, K), BF16),
            pltpu.VMEM((D, rows), BF16),
            pltpu.VMEM((D, rows), BF16),
            pltpu.VMEM((NX, NC, TILES, 8, 128), F32),
            pltpu.VMEM((NX, TILES, 8, 128), F32),
            pltpu.VMEM((NX, TILES, 8, 128), F32),
            pltpu.VMEM((NX - 1, TILES, 8, 128), F32),
            pltpu.VMEM((PER_Z * NZ, 8, 128), F32),
            pltpu.VMEM((NZ - 1, PER_Z, 8, 128), F32),
            pltpu.VMEM((NY, NX, NC, PER_Z * NZ, 8, 128), F32),
            pltpu.VMEM(square, F32),
            pltpu.VMEM(square, BF16),
            pltpu.VMEM(square, BF16),
            pltpu.VMEM(square, F32),
            pltpu.VMEM(square, BF16),
            pltpu.VMEM(square, BF16),
            pltpu.VMEM(square, BF16),
            pltpu.VMEM(square, BF16),
            pltpu.VMEM((OWN_M * K, rows), BF16),
            pltpu.VMEM((K, rows), BF16),
            pltpu.VMEM((NX * NC, ROWS_K, K), F32),
            pltpu.VMEM((NX * NC - 1, ROWS_K, K), F32),
            pltpu.VMEM((NZ, 8, K), F32),
            pltpu.VMEM((NZ - 1, 8, K), F32),
            pltpu.SemaphoreType.DMA((copies,)),
            pltpu.SemaphoreType.DMA((copies,)),
            pltpu.SemaphoreType.DMA((4,)),
        ],
        compiler_params=pltpu.CompilerParams(
            collective_id=0, has_side_effects=True, vmem_limit_bytes=56 * 2**20
        ),
        name="rotate_and_refit",
    )(vectors, codes, codebook.T.reshape(2, OWN // 2, K))
    return pl.pallas_call(
        finish_kernel,
        out_shape=(
            jax.ShapeDtypeStruct((OWN, D), F32),
            jax.ShapeDtypeStruct((K // (NX * NZ * NC), OWN), F32),
        ),
        in_specs=[vmem, vmem],
        out_specs=(vmem, vmem),
        name="finish",
    )(rotation, totals)


def solution(mesh):
    placed = (P("dim", "dp"), P("dim", "dp"), P(None, "dim"))
    return jax.shard_map(
        per_device,
        mesh=mesh,
        in_specs=placed,
        out_specs=(P("dim", None), P("dp", "dim")),
        check_vma=False,
    )
```
